256 devices in a mesh: expert: 64 (over x, y, z_hi), hidden: 4 (over z_lo, core).
Axes of the slice: x: 4, y: 4, z: 8 (z_hi: 4, z_lo: 2; z = z_hi * 2 + z_lo), core: 2. Of those that a mesh axis runs over, the one named last changes fastest.
Arguments:
- tokens: bfloat16 [256, 196, 1024], P('expert'), may hold values from -32 to 32
- slot_keys: bfloat16 [1024, 128], replicated, may hold values from -1 to 1
- w_in: bfloat16 [128, 1024, 4096], P('expert', None, 'hidden'), may hold values from -0.1875 to 0.1875
- b_in: float32 [128, 4096], P('expert', 'hidden'), may hold values from -6 to 6
- w_out: bfloat16 [128, 4096, 1024], P('expert', 'hidden'), may hold values from -0.09375 to 0.09375
- b_out: float32 [128, 1024], replicated, may hold values from -6 to 6
- out_grad: bfloat16 [256, 196, 1024], P('expert'), may hold values from -6 to 6
Outputs:
- token_grad: bfloat16 [256, 196, 1024], P(('expert', 'hidden'))
The draws below stay inside these ranges and needn't reach their ends.
All inputs are finite; a program needn't handle non-finite values.
Results may differ from the reference program's by a relative error of at most 0.028.
Values may be sent and summed in bfloat16 or wider, within the bound.
A program may use at most 64 MiB of HBM per device.

```python
import math
import jax
import jax.numpy as jnp
from jax import lax

D = 1024
FF = 4096
M = 196
EXPERTS = 128
IMAGES = 256
N_HIDDEN = 4


def make_keys(key):
    base = jax.random.normal(jax.random.fold_in(key, 11), (D, EXPERTS), jnp.float32) * (3.0 / math.sqrt(D))
    return jnp.clip(base, -1.0, 1.0)


def draw_slot_keys(key, part):
    return make_keys(key).astype(jnp.bfloat16)


def draw_tokens(key, part):
    base = jnp.clip(jax.random.normal(jax.random.fold_in(key, 21), (IMAGES, M, D), jnp.float32), -6.0, 6.0)
    return jnp.clip(base, -32.0, 32.0).astype(jnp.bfloat16)


def block_levels(own_key, dims, pieces, smallest, largest):
    def one(dim, parts):
        heights = jax.random.uniform(jax.random.fold_in(jax.random.fold_in(own_key, 6), dim), (parts,), jnp.float32, smallest / len(pieces), largest / len(pieces))
        return jnp.repeat(jnp.exp(heights), dims[dim] // parts).reshape((-1,) + (1,) * (len(dims) - dim - 1))

    gain = one(*pieces[0])
    for cut in pieces[1:]:
        gain = gain * one(*cut)
    return gain


def normal_values(rng, shape, scale, limit, shards=(), dtype=jnp.bfloat16):
    level = block_levels(rng, shape, shards, -0.22, 0.18) if shards else 1.0
    array = jax.random.normal(rng, shape, jnp.float32) * scale * level
    return jnp.minimum(jnp.maximum(array, -limit), limit).astype(dtype)


def setup_inputs(seed: int = 0) -> dict:
    seeds = jax.random.split(jax.random.key(seed), 8)
    tokens = draw_tokens(jax.random.fold_in(seeds[7], 71), 0)
    slot_keys = draw_slot_keys(jax.random.fold_in(seeds[7], 71), 0)
    w_in = normal_values(seeds[2], (EXPERTS, D, FF), D ** -0.5, 0.1875, ((0, 64), (2, 4)))
    b_in = normal_values(seeds[3], (EXPERTS, FF), 1.0, 6.0, ((0, 64), (1, 4)), jnp.float32)
    w_out = normal_values(seeds[4], (EXPERTS, FF, D), FF ** -0.5, 0.09375, ((0, 64), (1, 4)))
    b_out = normal_values(seeds[5], (EXPERTS, D), 1.0, 6.0, (), jnp.float32)
    out_grad = normal_values(seeds[6], (IMAGES, M, D), 1.0, 6.0, ((0, 64),))
    return dict(tokens=tokens, slot_keys=slot_keys, w_in=w_in, b_in=b_in, w_out=w_out, b_out=b_out, out_grad=out_grad)


def gelu_slope(pre_act):
    return 0.5 * (1.0 + lax.erf(pre_act * 0.7071067811865476)) + pre_act * jnp.exp(-0.5 * pre_act * pre_act) * 0.3989422804014327


def quarter_total(partials):
    rounded = partials.astype(jnp.bfloat16)
    rounded = lax.optimization_barrier(rounded)
    return jnp.sum(rounded.astype(jnp.float32), axis=0)


def expert_pass(operands):
    rows_in, rows_grad, weight_in, bias_in, weight_out, bias_out = operands
    batch = rows_in.shape[0]
    width = rows_in.shape[1]
    quarter_units = weight_in.shape[1] // N_HIDDEN
    pre_act = jnp.dot(rows_in, weight_in, preferred_element_type=jnp.float32) + bias_in
    hidden_act = jax.nn.gelu(pre_act, approximate=False).astype(jnp.bfloat16)
    out_parts = jnp.einsum("bqf,qfd->qbd", hidden_act.reshape(batch, N_HIDDEN, quarter_units).astype(jnp.float32), weight_out.reshape(N_HIDDEN, quarter_units, width).astype(jnp.float32))
    slot_out = (quarter_total(out_parts) + bias_out).astype(jnp.bfloat16)
    act_grad = jnp.dot(rows_grad, weight_out.T, preferred_element_type=jnp.float32)
    pre_grad = (act_grad * gelu_slope(pre_act)).astype(jnp.bfloat16)
    in_parts = jnp.einsum("bqf,dqf->qbd", pre_grad.reshape(batch, N_HIDDEN, quarter_units).astype(jnp.float32), weight_in.reshape(width, N_HIDDEN, quarter_units).astype(jnp.float32))
    slot_in_grad = quarter_total(in_parts).astype(jnp.bfloat16)
    return slot_out, slot_in_grad


def reference(tokens, slot_keys, w_in, b_in, w_out, b_out, out_grad):
    tokens_wide = tokens.astype(jnp.float32)
    keys_wide = slot_keys.astype(jnp.float32)
    grad_wide = out_grad.astype(jnp.float32)
    logits = jnp.einsum("btd,ds->bts", tokens_wide, keys_wide)
    dispatch = jax.nn.softmax(logits, axis=1).astype(jnp.bfloat16)
    combine = jax.nn.softmax(logits, axis=2).astype(jnp.bfloat16)
    disp_wide = dispatch.astype(jnp.float32)
    comb_wide = combine.astype(jnp.float32)
    slot_in = jnp.einsum("bts,btd->bsd", disp_wide, tokens_wide).astype(jnp.bfloat16)
    slot_grad = jnp.einsum("bts,btd->bsd", comb_wide, grad_wide).astype(jnp.bfloat16)
    per_expert = (jnp.swapaxes(slot_in, 0, 1), jnp.swapaxes(slot_grad, 0, 1), w_in, b_in, w_out, b_out)
    slot_out, slot_in_grad = lax.map(expert_pass, per_expert)
    slot_out = jnp.swapaxes(slot_out, 0, 1).astype(jnp.float32)
    slot_in_grad = jnp.swapaxes(slot_in_grad, 0, 1).astype(jnp.float32)
    comb_grad = jnp.einsum("btd,bsd->bts", grad_wide, slot_out)
    disp_grad = jnp.einsum("btd,bsd->bts", tokens_wide, slot_in_grad)
    logit_grad = comb_wide * (comb_grad - jnp.sum(comb_wide * comb_grad, axis=2, keepdims=True))
    logit_grad = logit_grad + disp_wide * (disp_grad - jnp.sum(disp_wide * disp_grad, axis=1, keepdims=True))
    logit_grad = logit_grad.astype(jnp.bfloat16).astype(jnp.float32)
    token_grad = jnp.einsum("bts,bsd->btd", disp_wide, slot_in_grad) + jnp.einsum("bts,ds->btd", logit_grad, keys_wide)
    return token_grad.astype(jnp.bfloat16)
```

```python
import functools

import jax
import jax.numpy as jnp
from jax import lax
from jax.experimental import pallas as pl
from jax.experimental.pallas import tpu as pltpu
from jax.sharding import PartitionSpec as P

BF = jnp.bfloat16
F32 = jnp.float32
MESH = pl.DeviceIdType.MESH
NT = (((1,), (1,)), ((), ()))
TN = (((0,), (0,)), ((), ()))


def mm(a, b):
    return jnp.dot(a, b, preferred_element_type=F32)


def nt(a, b):
    return lax.dot_general(a, b, NT, preferred_element_type=F32)


def tn(a, b):
    return lax.dot_general(a, b, TN, preferred_element_type=F32)


def onehot(shape, test):
    rows = lax.broadcasted_iota(jnp.int32, shape, 0)
    cols = lax.broadcasted_iota(jnp.int32, shape, 1)
    return jnp.where(test(rows, cols), 1.0, 0.0)


def kernel(
    tok_h, grad_h, keys_h, win_h, bin_h, wout_h, bout_h,
    out_ref,
    tok4, grad4, tok, grad, keys, win, wout, bin_, bout,
    send, rows0, rows1, slope, inter, part, fromcore, frompair, home,
    own_tok, own_grad, own_disp, own_comb, comb_all,
    load_sem, put_sem, got_sem, self_sem, fwd_sem, fgot_sem, cput_sem, cgot_sem,
    rput_sem, rgot_sem, zput_sem, zgot_sem, hput_sem, hgot_sem, hself_sem,
):
    e = lax.axis_index("expert")
    h = lax.axis_index("hidden")
    x, y, p = e // 16, (e // 4) % 4, e % 4
    zl, c = h // 2, h % 2
    n_slots, positions = 64, tok4.shape[0]
    rows_all = positions * 4
    rows = (rows0, rows1)

    def expert_at(dx, dy, dp):
        return ((x + dx) % 4) * 16 + ((y + dy) % 4) * 4 + (p + dp) % 4

    loads = [
        pltpu.make_async_copy(src, dst, load_sem.at[i])
        for i, (src, dst) in enumerate((
            (tok_h, tok4), (keys_h, keys), (grad_h, grad4), (win_h, win), (bin_h, bin_),
            (wout_h, wout), (bout_h, bout),
        ))
    ]
    for copy in loads:
        copy.start()

    barrier = pltpu.get_barrier_semaphore()

    def greet(expert, hidden):
        pl.semaphore_signal(barrier, inc=1, device_id=(expert, hidden), device_id_type=MESH)

    def greet_step(i, carry):
        dx, dy = i // 4, i % 4
        greet(expert_at(dx, dy, 1), c)
        greet(expert_at(dx, dy, 3), 2 + c)
        greet(expert_at(dx, dy, 2), 2 * (1 - zl) + c)
        return carry

    def greet_own(i, carry):
        greet(expert_at(i // 4, i % 4, 0), h)
        return carry

    lax.fori_loop(0, 16, greet_step, 0)
    lax.fori_loop(1, 16, greet_own, 0)
    greet(e, 2 * (1 - zl) + c)
    greet(e, 2 * zl + 1 - c)

    loads[0].wait()
    loads[1].wait()
    tok[...] = tok4[...].reshape(rows_all, tok4.shape[2])
    logits = mm(tok[...], keys[...])
    folded = logits.reshape(rows_all // 8, 8, logits.shape[1])
    top = jnp.max(folded, axis=0)
    top = jnp.maximum(top, pltpu.roll(top, 4, 0))
    weight = jnp.exp(folded - top[None])
    total = jnp.sum(weight, axis=0)
    total = total + pltpu.roll(total, 4, 0)
    dispatch = (weight / total[None]).reshape(rows_all, logits.shape[1]).astype(BF)
    weight = jnp.exp(logits - jnp.max(logits, axis=1, keepdims=True))
    combine = (weight / jnp.sum(weight, axis=1, keepdims=True)).astype(BF)
    comb_all[...] = combine
    spread = onehot((128, 256), lambda r, q: q // 2 == r).astype(BF)
    image = lax.broadcasted_iota(jnp.int32, (rows_all, 256), 0) % 4
    wanted = c + 2 * (lax.broadcasted_iota(jnp.int32, (rows_all, 256), 1) % 2)

    def slots(scores, values):
        wide = jnp.where(image == wanted, mm(scores, spread), 0.0).astype(BF)
        return tn(wide, values).astype(BF).reshape(64, 2, 2, values.shape[1])

    def put(t, expert, hidden, slot, group):
        return pltpu.make_async_remote_copy(
            src_ref=send.at[t, expert], dst_ref=rows[t].at[c, slot],
            send_sem=put_sem.at[t], recv_sem=got_sem.at[t, group],
            device_id=(expert, hidden), device_id_type=MESH,
        )

    def odd_even(b, par):
        dx = b // 2
        return dx, 2 * (b % 2) + (dx + par) % 2

    def send_all(t):
        def far(b, carry):
            dx, dy = odd_even(b, 1 - zl)
            put(t, expert_at(dx, dy, 2), 2 * (1 - zl) + c, 16 + 8 * (1 - zl) + b, 1).start()
            return carry

        def near(i, carry):
            put(t, expert_at(i // 4, i % 4, 3 - 2 * zl), 2 * (1 - zl) + c, 32 * (1 - zl) + i, 0).start()
            return carry

        def level(i, carry):
            put(t, expert_at(i // 4, i % 4, 0), h, 48 + i, 2).start()
            return carry

        pltpu.make_async_copy(send.at[t, e], rows[t].at[c, 48], self_sem.at[t]).start()
        lax.fori_loop(0, 8, far, 0)
        lax.fori_loop(0, 16, near, 0)
        lax.fori_loop(1, 16, level, 0)

    def wait_for(ref, sem):
        pltpu.make_async_copy(ref, ref, sem).wait()

    send[0] = slots(dispatch, tok[...])
    pl.semaphore_wait(barrier, 65)
    send_all(0)
    loads[2].wait()
    grad[...] = grad4[...].reshape(rows_all, grad4.shape[2])
    send[1] = slots(comb_all[...], grad[...])
    send_all(1)

    pick = onehot((positions, rows_all), lambda r, q: q == 4 * r + h).astype(BF)
    own_tok[...] = mm(pick, tok[...]).astype(BF)
    own_grad[...] = mm(pick, grad[...]).astype(BF)
    own_disp[...] = mm(pick, dispatch)
    own_comb[...] = mm(pick, comb_all[...])
    for copy in loads[3:]:
        copy.wait()

    pair = (e, 2 * (1 - zl) + c)
    mate = (e, 2 * zl + 1 - c)
    base_a = 32 * zl
    base_b = 16 + 8 * zl
    pair_a = 32 * (1 - zl)
    pair_b = 16 + 8 * (1 - zl)

    def share(t, which, start, count):
        piece = rows[t].at[c, pl.ds(start, count)]
        pltpu.make_async_remote_copy(
            src_ref=piece, dst_ref=piece, send_sem=cput_sem.at[t, which], recv_sem=cgot_sem.at[t, which],
            device_id=mate, device_id_type=MESH,
        ).start()

    def forward(t, which, start, count):
        piece = rows[t].at[c, pl.ds(start, count)]
        pltpu.make_async_remote_copy(
            src_ref=piece, dst_ref=piece, send_sem=fwd_sem.at[t, which], recv_sem=fgot_sem.at[t, which],
            device_id=pair, device_id_type=MESH,
        ).start()

    def gather_rows(t):
        wait_for(rows[t].at[c, pl.ds(base_b, 8)], got_sem.at[t, 1])
        forward(t, 1, base_b, 8)
        share(t, 1, base_b, 8)
        wait_for(rows[t].at[c, pl.ds(base_a, 16)], got_sem.at[t, 0])
        forward(t, 0, base_a, 16)
        share(t, 0, base_a, 16)
        wait_for(rows[t].at[c, pl.ds(49, 15)], got_sem.at[t, 2])
        pltpu.make_async_copy(send.at[t, e], rows[t].at[c, 48], self_sem.at[t]).wait()
        share(t, 2, 48, 16)
        wait_for(rows[t].at[c, pl.ds(pair_b, 8)], fgot_sem.at[t, 1])
        share(t, 3, pair_b, 8)
        wait_for(rows[t].at[c, pl.ds(pair_a, 16)], fgot_sem.at[t, 0])
        share(t, 4, pair_a, 16)
        wait_for(rows[t].at[c, pl.ds(0, 8)], cgot_sem.at[t, 1])
        wait_for(rows[t].at[c, pl.ds(0, 16)], cgot_sem.at[t, 0])
        wait_for(rows[t].at[c, pl.ds(0, 16)], cgot_sem.at[t, 2])
        wait_for(rows[t].at[c, pl.ds(0, 8)], cgot_sem.at[t, 3])
        wait_for(rows[t].at[c, pl.ds(0, 16)], cgot_sem.at[t, 4])

    width = tok4.shape[2]

    def expert_rows(t, k):
        return rows[t][:, :, k].reshape(256, width)

    def core_copy(t):
        return pltpu.make_async_remote_copy(
            src_ref=part.at[t, 1 - c], dst_ref=fromcore.at[t], send_sem=rput_sem.at[t], recv_sem=rgot_sem.at[t],
            device_id=mate, device_id_type=MESH,
        )

    def pair_copies(t):
        sent = (
            part.at[t, c, pl.ds(32 * (1 - zl), 16)],
            part.at[t, c, pl.ds(16, 16), pl.ds(zl, 1)],
            part.at[t, c, pl.ds(48, 16), pl.ds(1 - zl, 1)],
        )
        land = (
            frompair.at[t, pl.ds(0, 16)],
            frompair.at[t, pl.ds(16, 16), pl.ds(0, 1)],
            frompair.at[t, pl.ds(16, 16), pl.ds(1, 1)],
        )
        return [
            pltpu.make_async_remote_copy(
                src_ref=s, dst_ref=d, send_sem=zput_sem.at[t, i], recv_sem=zgot_sem.at[t, i],
                device_id=pair, device_id_type=MESH,
            )
            for i, (s, d) in enumerate(zip(sent, land))
        ]

    def add_core(t):
        core_copy(t).wait_recv()
        mine = part[t, c]
        part[t, c] = (mine.astype(F32) + fromcore[t].astype(F32)).astype(BF)

    def add_pair(t):
        for copy in pair_copies(t):
            copy.wait_recv()
        first = part[t, c, pl.ds(32 * zl, 16)].astype(F32)
        frompair[t, 0:16] = (frompair[t, 0:16].astype(F32) + first).astype(BF)
        second = part[t, c, 16:32, pl.ds(1 - zl, 1)].astype(F32)
        frompair[t, 16:32, 0:1] = (frompair[t, 16:32, 0:1].astype(F32) + second).astype(BF)
        third = part[t, c, 48:64, pl.ds(zl, 1)].astype(F32)
        frompair[t, 16:32, 1:2] = (frompair[t, 16:32, 1:2].astype(F32) + third).astype(BF)

    def go_home(t):
        def put_home(slot, j, expert, hidden):
            pltpu.make_async_remote_copy(
                src_ref=frompair.at[t, slot, j], dst_ref=home.at[t, e], send_sem=hput_sem.at[t],
                recv_sem=hgot_sem.at[t], device_id=(expert, hidden), device_id_type=MESH,
            ).start()

        def far(b, carry):
            for par in (0, 1):
                dx, dy = odd_even(b, par)
                put_home(16 + 8 * par + b, 0, expert_at(4 - dx, 4 - dy, 2), 2 * (1 - zl) + c)
            return carry

        def near(i, carry):
            expert = expert_at(4 - i // 4, 4 - i % 4, 3 - 2 * zl)
            put_home(i, 0, expert, c)
            put_home(i, 1, expert, 2 + c)
            return carry

        def level(i, carry):
            put_home(16 + i, 1, expert_at(4 - i // 4, 4 - i % 4, 0), h)
            return carry

        pltpu.make_async_copy(frompair.at[t, 16, 1], home.at[t, e], hself_sem.at[t]).start()
        lax.fori_loop(0, 8, far, 0)
        lax.fori_loop(0, 16, near, 0)
        lax.fori_loop(1, 16, level, 0)

    def interleave(k, product):
        for n in range(width // 128):
            inter[n, pl.ds(k, 256, 2), :] = product[:, 128 * n : 128 * n + 128]

    def pack(t):
        both = jnp.concatenate([inter[n] for n in range(width // 128)], axis=1)
        part[t] = both.astype(BF).reshape(2, n_slots, 2, 2, width)

    gather_rows(0)
    for k in range(2):
        pre = mm(expert_rows(0, k), win[k]) + bin_[k : k + 1]
        half = 0.5 * (1.0 + lax.erf(pre * 0.7071067811865476))
        slope[k] = half + pre * jnp.exp(-0.5 * pre * pre) * 0.3989422804014327
        interleave(k, mm((pre * half).astype(BF), wout[k]))
    pack(0)
    core_copy(0).start()
    add_core(0)
    for copy in pair_copies(0):
        copy.start()

    gather_rows(1)
    add_pair(0)
    go_home(0)
    for k in range(2):
        pre_grad = (nt(expert_rows(1, k), wout[k]) * slope[k]).astype(BF)
        interleave(k, nt(pre_grad, win[k]))
    pack(1)
    core_copy(1).start()
    add_core(1)
    for copy in pair_copies(1):
        copy.start()
    add_pair(1)
    go_home(1)

    def wait_home(t):
        wait_for(home.at[t, pl.ds(0, 63)], hgot_sem.at[t])
        pltpu.make_async_copy(frompair.at[t, 16, 1], home.at[t, e], hself_sem.at[t]).wait()

    wait_home(0)
    slot_out = (home[0].reshape(128, width).astype(F32) + bout[...]).astype(BF)
    comb = own_comb[...]
    disp = own_disp[...]
    comb_grad = nt(own_grad[...], slot_out)
    comb_term = comb * (comb_grad - jnp.sum(comb * comb_grad, axis=1, keepdims=True))
    wait_home(1)
    slot_in_grad = home[1].reshape(128, width)
    disp_grad = nt(own_tok[...], slot_in_grad)
    logit_grad = comb_term + disp * (disp_grad - jnp.sum(disp * disp_grad, axis=0, keepdims=True))
    result = mm(disp.astype(BF), slot_in_grad) + nt(logit_grad.astype(BF), keys[...])
    out_ref[...] = result.astype(BF)

    for t in range(2):
        wait_for(send.at[t, pl.ds(0, 39)], put_sem.at[t])
        wait_for(rows[t].at[0, pl.ds(0, 16)], fwd_sem.at[t, 0])
        wait_for(rows[t].at[0, pl.ds(0, 8)], fwd_sem.at[t, 1])
        for which, count in enumerate((16, 8, 16, 8, 16)):
            wait_for(rows[t].at[0, pl.ds(0, count)], cput_sem.at[t, which])
        core_copy(t).wait_send()
        for copy in pair_copies(t):
            copy.wait_send()
        wait_for(home.at[t, pl.ds(0, 63)], hput_sem.at[t])


def local(tokens, slot_keys, w_in, b_in, w_out, b_out, out_grad):
    images, positions, width = tokens.shape
    units = w_in.shape[2]
    slots = slot_keys.shape[1]
    anyspec = pl.BlockSpec(memory_space=pl.ANY)
    dma = pltpu.SemaphoreType.DMA
    out = pl.pallas_call(
        kernel,
        out_shape=jax.ShapeDtypeStruct((positions, width), BF),
        in_specs=[anyspec] * 7,
        out_specs=pl.BlockSpec(memory_space=pltpu.VMEM),
        scratch_shapes=[
            pltpu.VMEM((positions, images, width), BF),
            pltpu.VMEM((positions, images, width), BF),
            pltpu.VMEM((positions * images, width), BF),
            pltpu.VMEM((positions * images, width), BF),
            pltpu.VMEM((width, slots), BF),
            pltpu.VMEM((2, width, units), BF),
            pltpu.VMEM((2, units, width), BF),
            pltpu.VMEM((2, units), F32),
            pltpu.VMEM((slots, width), F32),
            pltpu.VMEM((2, 64, 2, 2, width), BF),
            pltpu.VMEM((2, 64, 2, 2, width), BF),
            pltpu.VMEM((2, 64, 2, 2, width), BF),
            pltpu.VMEM((2, 256, units), F32),
            pltpu.VMEM((width // 128, 512, 128), F32),
            pltpu.VMEM((2, 2, 64, 2, 2, width), BF),
            pltpu.VMEM((2, 64, 2, 2, width), BF),
            pltpu.VMEM((2, 32, 2, 2, width), BF),
            pltpu.VMEM((2, 64, 2, width), BF),
            pltpu.VMEM((positions, width), BF),
            pltpu.VMEM((positions, width), BF),
            pltpu.VMEM((positions, slots), F32),
            pltpu.VMEM((positions, slots), F32),
            pltpu.VMEM((positions * images, slots), BF),
            dma((7,)), dma((2,)), dma((2, 3)), dma((2,)), dma((2, 2)), dma((2, 2)), dma((2, 5)), dma((2, 5)),
            dma((2,)), dma((2,)), dma((2, 3)), dma((2, 3)), dma((2,)), dma((2,)), dma((2,)),
        ],
        compiler_params=pltpu.CompilerParams(
            collective_id=0, has_side_effects=True, vmem_limit_bytes=58 * 1024 * 1024
        ),
        name="moe_input_grad",
    )(
        jnp.transpose(tokens, (1, 0, 2)), jnp.transpose(out_grad, (1, 0, 2)), slot_keys, w_in, b_in, w_out, b_out
    )
    return out[None]


def solution(mesh):
    return jax.shard_map(
        local,
        mesh=mesh,
        in_specs=(
            P("expert", None, None),
            P(),
            P("expert", None, "hidden"),
            P("expert", "hidden"),
            P("expert", "hidden", None),
            P(),
            P("expert", None, None),
        ),
        out_specs=P(("expert", "hidden"), None, None),
        check_vma=False,
    )
```

```python
import functools

import jax
import jax.numpy as jnp
from jax import lax
from jax.experimental import pallas as pl
from jax.experimental.pallas import tpu as pltpu
from jax.sharding import PartitionSpec as P

BF = jnp.bfloat16
F32 = jnp.float32
MESH = pl.DeviceIdType.MESH
NT = (((1,), (1,)), ((), ()))
TN = (((0,), (0,)), ((), ()))


def mm(a, b):
    return jnp.dot(a, b, preferred_element_type=F32)


def nt(a, b):
    return lax.dot_general(a, b, NT, preferred_element_type=F32)


def tn(a, b):
    return lax.dot_general(a, b, TN, preferred_element_type=F32)


def onehot(shape, test):
    rows = lax.broadcasted_iota(jnp.int32, shape, 0)
    cols = lax.broadcasted_iota(jnp.int32, shape, 1)
    return jnp.where(test(rows, cols), 1.0, 0.0)


def kernel(
    tok_h, grad_h, keys_h, win_h, bin_h, wout_h, bout_h,
    out_ref,
    tok4, grad4, tok, grad, keys, win, wout, bin_, bout,
    send, rows0, rows1, slope, act, inter, part, fromcore, frompair, home,
    own_tok, own_grad, own_disp, own_comb, comb_all,
    load_sem, put_sem, got_sem, self_sem, fwd_sem, fgot_sem, cput_sem, cgot_sem,
    rput_sem, rgot_sem, zput_sem, zgot_sem, hput_sem, hgot_sem, hself_sem,
):
    e = lax.axis_index("expert")
    h = lax.axis_index("hidden")
    x, y, p = e // 16, (e // 4) % 4, e % 4
    zl, c = h // 2, h % 2
    n_slots, positions = 64, tok4.shape[0]
    rows_all = positions * 4
    rows = (rows0, rows1)

    def expert_at(dx, dy, dp):
        return ((x + dx) % 4) * 16 + ((y + dy) % 4) * 4 + (p + dp) % 4

    loads = [
        pltpu.make_async_copy(src, dst, load_sem.at[i])
        for i, (src, dst) in enumerate((
            (tok_h, tok4), (keys_h, keys), (grad_h, grad4), (win_h, win), (bin_h, bin_),
            (wout_h, wout), (bout_h, bout),
        ))
    ]
    for copy in loads:
        copy.start()

    barrier = pltpu.get_barrier_semaphore()

    def greet(expert, hidden):
        pl.semaphore_signal(barrier, inc=1, device_id=(expert, hidden), device_id_type=MESH)

    def greet_step(i, carry):
        dx, dy = i // 4, i % 4
        greet(expert_at(dx, dy, 1), c)
        greet(expert_at(dx, dy, 3), 2 + c)
        greet(expert_at(dx, dy, 2), 2 * (1 - zl) + c)
        return carry

    def greet_own(i, carry):
        greet(expert_at(i // 4, i % 4, 0), h)
        return carry

    lax.fori_loop(0, 16, greet_step, 0)
    lax.fori_loop(1, 16, greet_own, 0)
    greet(e, 2 * (1 - zl) + c)
    greet(e, 2 * zl + 1 - c)

    loads[0].wait()
    loads[1].wait()
    tok[...] = tok4[...].reshape(rows_all, tok4.shape[2])
    logits = mm(tok[...], keys[...])
    folded = logits.reshape(rows_all // 8, 8, logits.shape[1])
    top = jnp.max(folded, axis=0)
    top = jnp.maximum(top, pltpu.roll(top, 4, 0))
    weight = jnp.exp(folded - top[None])
    total = jnp.sum(weight, axis=0)
    total = total + pltpu.roll(total, 4, 0)
    dispatch = (weight / total[None]).reshape(rows_all, logits.shape[1]).astype(BF)
    weight = jnp.exp(logits - jnp.max(logits, axis=1, keepdims=True))
    combine = (weight / jnp.sum(weight, axis=1, keepdims=True)).astype(BF)
    comb_all[...] = combine
    spread = onehot((128, 256), lambda r, q: q // 2 == r).astype(BF)
    image = lax.broadcasted_iota(jnp.int32, (rows_all, 256), 0) % 4
    wanted = c + 2 * (lax.broadcasted_iota(jnp.int32, (rows_all, 256), 1) % 2)

    def slots(scores, values):
        wide = jnp.where(image == wanted, mm(scores, spread), 0.0).astype(BF)
        return tn(wide, values).astype(BF).reshape(64, 2, 2, values.shape[1])

    def put(t, expert, hidden, slot, piece):
        return pltpu.make_async_remote_copy(
            src_ref=send.at[t, expert], dst_ref=rows[t].at[c, slot],
            send_sem=put_sem.at[t], recv_sem=got_sem.at[t, piece],
            device_id=(expert, hidden), device_id_type=MESH,
        )

    def odd_even(b, par):
        dx = b // 2
        return dx, 2 * (b % 2) + (dx + par) % 2

    def send_all(t):
        def far(b, carry):
            dx, dy = odd_even(b, 1 - zl)
            put(t, expert_at(dx, dy, 2), 2 * (1 - zl) + c, 16 + 8 * (1 - zl) + b, 0).start()
            return carry

        def near(piece, i, carry):
            put(t, expert_at(i // 4, i % 4, 3 - 2 * zl), 2 * (1 - zl) + c, 32 * (1 - zl) + i, piece).start()
            return carry

        def level(i, carry):
            put(t, expert_at(i // 4, i % 4, 0), h, 48 + i, 3).start()
            return carry

        pltpu.make_async_copy(send.at[t, e], rows[t].at[c, 48], self_sem.at[t]).start()
        lax.fori_loop(0, 8, far, 0)
        lax.fori_loop(0, 8, functools.partial(near, 1), 0)
        lax.fori_loop(8, 16, functools.partial(near, 2), 0)
        lax.fori_loop(1, 16, level, 0)

    def wait_for(ref, sem):
        pltpu.make_async_copy(ref, ref, sem).wait()

    send[0] = slots(dispatch, tok[...])
    pl.semaphore_wait(barrier, 65)
    send_all(0)
    loads[2].wait()
    grad[...] = grad4[...].reshape(rows_all, grad4.shape[2])
    send[1] = slots(comb_all[...], grad[...])
    send_all(1)

    pick = onehot((positions, rows_all), lambda r, q: q == 4 * r + h).astype(BF)
    own_tok[...] = mm(pick, tok[...]).astype(BF)
    own_grad[...] = mm(pick, grad[...]).astype(BF)
    own_disp[...] = mm(pick, dispatch)
    own_comb[...] = mm(pick, comb_all[...])
    for copy in loads[3:]:
        copy.wait()

    pair = (e, 2 * (1 - zl) + c)
    mate = (e, 2 * zl + 1 - c)
    starts = (
        16 + 8 * zl, 32 * zl, 32 * zl + 8, 48,
        16 + 8 * (1 - zl), 32 * (1 - zl), 32 * (1 - zl) + 8,
    )
    counts = (8, 8, 8, 16, 8, 8, 8)

    def piece_ref(t, i):
        return rows[t].at[c, pl.ds(starts[i], counts[i])]

    def share(t, i):
        pltpu.make_async_remote_copy(
            src_ref=piece_ref(t, i), dst_ref=piece_ref(t, i), send_sem=cput_sem.at[t, i],
            recv_sem=cgot_sem.at[t, i], device_id=mate, device_id_type=MESH,
        ).start()

    def forward(t, i):
        pltpu.make_async_remote_copy(
            src_ref=piece_ref(t, i), dst_ref=piece_ref(t, i), send_sem=fwd_sem.at[t, i],
            recv_sem=fgot_sem.at[t, i], device_id=pair, device_id_type=MESH,
        ).start()

    def take(t, i):
        if i == 3:
            wait_for(rows[t].at[c, pl.ds(49, 15)], got_sem.at[t, 3])
            pltpu.make_async_copy(send.at[t, e], rows[t].at[c, 48], self_sem.at[t]).wait()
        elif i < 3:
            wait_for(piece_ref(t, i), got_sem.at[t, i])
            forward(t, i)
        else:
            wait_for(piece_ref(t, i), fgot_sem.at[t, i - 4])
        share(t, i)

    def complete(t):
        for i, count in enumerate(counts):
            wait_for(rows[t].at[c, pl.ds(0, count)], cgot_sem.at[t, i])

    width = tok4.shape[2]

    def expert_rows(t, k):
        return rows[t][:, :, k].reshape(256, width)

    def gone(k):
        return (
            (pl.ds(16, 16), pl.ds(zl, 1)), (pl.ds(32 * (1 - zl), 8), pl.ds(0, 2)),
            (pl.ds(32 * (1 - zl) + 8, 8), pl.ds(0, 2)), (pl.ds(48, 16), pl.ds(1 - zl, 1)),
        )[k]

    def kept(k):
        return (
            (pl.ds(16, 16), pl.ds(1 - zl, 1)), (pl.ds(32 * zl, 8), pl.ds(0, 2)),
            (pl.ds(32 * zl + 8, 8), pl.ds(0, 2)), (pl.ds(48, 16), pl.ds(zl, 1)),
        )[k]

    landing = (
        (pl.ds(16, 16), pl.ds(0, 1)), (pl.ds(0, 8), pl.ds(0, 2)),
        (pl.ds(8, 8), pl.ds(0, 2)), (pl.ds(16, 16), pl.ds(1, 1)),
    )

    def to_core(t):
        for half, pieces in enumerate((gone, kept)):
            for k in range(4):
                s, j = pieces(k)
                pltpu.make_async_remote_copy(
                    src_ref=part.at[t, 1 - c, s, j], dst_ref=fromcore.at[t, s, j], send_sem=rput_sem.at[t],
                    recv_sem=rgot_sem.at[t, half], device_id=mate, device_id_type=MESH,
                ).start()

    def add_core(t, half):
        wait_for(fromcore.at[t, pl.ds(0, 32)], rgot_sem.at[t, half])
        for k in range(4):
            s, j = (gone, kept)[half](k)
            part[t, c, s, j] = (part[t, c, s, j].astype(F32) + fromcore[t, s, j].astype(F32)).astype(BF)

    def to_pair(t, k):
        s, j = gone(k)
        ls, lj = landing[k]
        return pltpu.make_async_remote_copy(
            src_ref=part.at[t, c, s, j], dst_ref=frompair.at[t, ls, lj], send_sem=zput_sem.at[t, k],
            recv_sem=zgot_sem.at[t, k], device_id=pair, device_id_type=MESH,
        )

    def pair_up(t):
        add_core(t, 0)
        for k in range(4):
            to_pair(t, k).start()

    def add_pair(t, k):
        to_pair(t, k).wait_recv()
        s, j = kept(k)
        ls, lj = landing[k]
        frompair[t, ls, lj] = (frompair[t, ls, lj].astype(F32) + part[t, c, s, j].astype(F32)).astype(BF)

    def go_home(t):
        def put_home(slot, j, expert, hidden):
            pltpu.make_async_remote_copy(
                src_ref=frompair.at[t, slot, j], dst_ref=home.at[t, e], send_sem=hput_sem.at[t],
                recv_sem=hgot_sem.at[t], device_id=(expert, hidden), device_id_type=MESH,
            ).start()

        def far(b, carry):
            for par in (0, 1):
                dx, dy = odd_even(b, par)
                put_home(16 + 8 * par + b, 0, expert_at(4 - dx, 4 - dy, 2), 2 * (1 - zl) + c)
            return carry

        def near(i, carry):
            expert = expert_at(4 - i // 4, 4 - i % 4, 3 - 2 * zl)
            put_home(i, 0, expert, c)
            put_home(i, 1, expert, 2 + c)
            return carry

        def level(i, carry):
            put_home(16 + i, 1, expert_at(4 - i // 4, 4 - i % 4, 0), h)
            return carry

        add_pair(t, 0)
        lax.fori_loop(0, 8, far, 0)
        add_pair(t, 1)
        lax.fori_loop(0, 8, near, 0)
        add_pair(t, 2)
        lax.fori_loop(8, 16, near, 0)
        add_pair(t, 3)
        pltpu.make_async_copy(frompair.at[t, 16, 1], home.at[t, e], hself_sem.at[t]).start()
        lax.fori_loop(1, 16, level, 0)

    def project(t, cc, product):
        for k in range(2):
            rows_k = product(k, act[k, pl.ds(pl.multiple_of(128 * cc, 128), 128)])
            for n in range(width // 128):
                inter[n, pl.ds(k, 128, 2), :] = rows_k[:, 128 * n : 128 * n + 128]
        both = jnp.concatenate([inter[n] for n in range(width // 128)], axis=1)
        part[t, cc] = both.astype(BF).reshape(n_slots, 2, 2, width)

    def reduce_first(t, product):
        project(t, 1 - c, product)
        to_core(t)
        project(t, c, product)

    take(0, 0)
    take(0, 1)
    take(0, 2)
    take(0, 3)
    take(0, 4)
    take(1, 0)
    take(0, 5)
    take(1, 1)
    take(0, 6)
    take(1, 2)
    take(1, 3)
    complete(0)
    for k in range(2):
        pre = mm(expert_rows(0, k), win[k]) + bin_[k : k + 1]
        half = 0.5 * (1.0 + lax.erf(pre * 0.7071067811865476))
        slope[k] = half + pre * jnp.exp(-0.5 * pre * pre) * 0.3989422804014327
        act[k] = (pre * half).astype(BF)
    reduce_first(0, lambda k, a: mm(a, wout[k]))
    pair_up(0)
    take(1, 4)
    take(1, 5)
    take(1, 6)
    add_core(0, 1)
    complete(1)
    for k in range(2):
        act[k] = (nt(expert_rows(1, k), wout[k]) * slope[k]).astype(BF)
    reduce_first(1, lambda k, a: nt(a, win[k]))
    go_home(0)
    pair_up(1)
    add_core(1, 1)
    go_home(1)

    def wait_home(t):
        wait_for(home.at[t, pl.ds(0, 63)], hgot_sem.at[t])
        pltpu.make_async_copy(frompair.at[t, 16, 1], home.at[t, e], hself_sem.at[t]).wait()

    wait_home(0)
    slot_out = (home[0].reshape(128, width).astype(F32) + bout[...]).astype(BF)
    comb = own_comb[...]
    disp = own_disp[...]
    comb_grad = nt(own_grad[...], slot_out)
    comb_term = comb * (comb_grad - jnp.sum(comb * comb_grad, axis=1, keepdims=True))
    wait_home(1)
    slot_in_grad = home[1].reshape(128, width)
    disp_grad = nt(own_tok[...], slot_in_grad)
    logit_grad = comb_term + disp * (disp_grad - jnp.sum(disp * disp_grad, axis=0, keepdims=True))
    result = mm(disp.astype(BF), slot_in_grad) + nt(logit_grad.astype(BF), keys[...])
    out_ref[...] = result.astype(BF)

    for t in range(2):
        wait_for(send.at[t, pl.ds(0, 39)], put_sem.at[t])
        for i in range(3):
            wait_for(rows[t].at[0, pl.ds(0, 8)], fwd_sem.at[t, i])
        for i, count in enumerate(counts):
            wait_for(rows[t].at[0, pl.ds(0, count)], cput_sem.at[t, i])
        wait_for(fromcore.at[t], rput_sem.at[t])
        for k in range(4):
            to_pair(t, k).wait_send()
        wait_for(home.at[t, pl.ds(0, 63)], hput_sem.at[t])


def local(tokens, slot_keys, w_in, b_in, w_out, b_out, out_grad):
    images, positions, width = tokens.shape
    units = w_in.shape[2]
    slots = slot_keys.shape[1]
    anyspec = pl.BlockSpec(memory_space=pl.ANY)
    dma = pltpu.SemaphoreType.DMA
    out = pl.pallas_call(
        kernel,
        out_shape=jax.ShapeDtypeStruct((positions, width), BF),
        in_specs=[anyspec] * 7,
        out_specs=pl.BlockSpec(memory_space=pltpu.VMEM),
        scratch_shapes=[
            pltpu.VMEM((positions, images, width), BF),
            pltpu.VMEM((positions, images, width), BF),
            pltpu.VMEM((positions * images, width), BF),
            pltpu.VMEM((positions * images, width), BF),
            pltpu.VMEM((width, slots), BF),
            pltpu.VMEM((2, width, units), BF),
            pltpu.VMEM((2, units, width), BF),
            pltpu.VMEM((2, units), F32),
            pltpu.VMEM((slots, width), F32),
            pltpu.VMEM((2, 64, 2, 2, width), BF),
            pltpu.VMEM((2, 64, 2, 2, width), BF),
            pltpu.VMEM((2, 64, 2, 2, width), BF),
            pltpu.VMEM((2, 256, units), F32),
            pltpu.VMEM((2, 256, units), BF),
            pltpu.VMEM((width // 128, 256, 128), F32),
            pltpu.VMEM((2, 2, 64, 2, 2, width), BF),
            pltpu.VMEM((2, 64, 2, 2, width), BF),
            pltpu.VMEM((2, 32, 2, 2, width), BF),
            pltpu.VMEM((2, 64, 2, width), BF),
            pltpu.VMEM((positions, width), BF),
            pltpu.VMEM((positions, width), BF),
            pltpu.VMEM((positions, slots), F32),
            pltpu.VMEM((positions, slots), F32),
            pltpu.VMEM((positions * images, slots), BF),
            dma((7,)), dma((2,)), dma((2, 4)), dma((2,)), dma((2, 3)), dma((2, 3)), dma((2, 7)), dma((2, 7)),
            dma((2,)), dma((2, 2)), dma((2, 4)), dma((2, 4)), dma((2,)), dma((2,)), dma((2,)),
        ],
        compiler_params=pltpu.CompilerParams(
            collective_id=0, has_side_effects=True, vmem_limit_bytes=58 * 1024 * 1024
        ),
        name="moe_input_grad",
    )(
        jnp.transpose(tokens, (1, 0, 2)), jnp.transpose(out_grad, (1, 0, 2)), slot_keys, w_in, b_in, w_out, b_out
    )
    return out[None]


def solution(mesh):
    return jax.shard_map(
        local,
        mesh=mesh,
        in_specs=(
            P("expert", None, None),
            P(),
            P("expert", None, "hidden"),
            P("expert", "hidden"),
            P("expert", "hidden", None),
            P(),
            P("expert", None, None),
        ),
        out_specs=P(("expert", "hidden"), None, None),
        check_vma=False,
    )
```

```python
import functools

import jax
import jax.numpy as jnp
from jax import lax
from jax.experimental import pallas as pl
from jax.experimental.pallas import tpu as pltpu
from jax.sharding import PartitionSpec as P

BF = jnp.bfloat16
F32 = jnp.float32
MESH = pl.DeviceIdType.MESH
NT = (((1,), (1,)), ((), ()))
TN = (((0,), (0,)), ((), ()))


def mm(a, b):
    return jnp.dot(a, b, preferred_element_type=F32)


def nt(a, b):
    return lax.dot_general(a, b, NT, preferred_element_type=F32)


def tn(a, b):
    return lax.dot_general(a, b, TN, preferred_element_type=F32)


def onehot(shape, test):
    rows = lax.broadcasted_iota(jnp.int32, shape, 0)
    cols = lax.broadcasted_iota(jnp.int32, shape, 1)
    return jnp.where(test(rows, cols), 1.0, 0.0)


def kernel(
    tok_h, grad_h, keys_h, win_h, bin_h, wout_h, bout_h,
    out_ref,
    tok4, grad4, tok, grad, keys, win, wout, bin_, bout,
    send, rows0, rows1, slope, act, inter, part, fromcore, frompair, home,
    own_tok, own_grad, own_disp, own_comb, comb_all, disp_all, scores, flipped,
    load_sem, put_sem, got_sem, self_sem, fwd_sem, fgot_sem, cput_sem, cgot_sem,
    rput_sem, rgot_sem, zput_sem, zgot_sem, hput_sem, hgot_sem, hself_sem,
):
    e = lax.axis_index("expert")
    h = lax.axis_index("hidden")
    x, y, p = e // 16, (e // 4) % 4, e % 4
    zl, c = h // 2, h % 2
    n_slots, positions = 64, tok4.shape[0]
    rows_all = positions * 4
    rows = (rows0, rows1)

    xs = [lax.rem(x + d, 4) * 16 for d in range(4)]
    ys = [lax.rem(y + d, 4) * 4 for d in range(4)]
    ps = [lax.rem(p + d, 4) for d in range(4)]
    ahead = lax.rem(p + 3 - 2 * zl, 4)
    offsets = (
        (0, 0), (1, 0), (0, 1), (3, 0), (0, 3), (1, 1), (3, 3), (1, 3),
        (3, 1), (2, 0), (0, 2), (2, 1), (1, 2), (2, 3), (3, 2), (2, 2),
    )

    def expert_at(dx, dy, plane):
        return xs[dx % 4] + ys[dy % 4] + plane

    def checkered(flip):
        return [(b // 2, 2 * (b % 2) + (b // 2 + flip) % 2) for b in range(8)]

    swapped = [lax.rem(y + d, 4) * 4 for d in (1 - zl, zl, 3 - zl, 2 + zl)]

    loads = [
        pltpu.make_async_copy(src, dst, load_sem.at[i])
        for i, (src, dst) in enumerate((
            (tok_h, tok4), (keys_h, keys), (grad_h, grad4), (win_h, win), (bin_h, bin_),
            (wout_h, wout), (bout_h, bout),
        ))
    ]
    loads[0].start()
    loads[1].start()

    barrier = pltpu.get_barrier_semaphore()

    def greet(expert, hidden):
        pl.semaphore_signal(barrier, inc=1, device_id=(expert, hidden), device_id_type=MESH)

    for dx, dy in offsets[::-1]:
        greet(expert_at(dx, dy, ps[2]), 2 * (1 - zl) + c)
        greet(expert_at(dx, dy, ps[1]), c)
        greet(expert_at(dx, dy, ps[3]), 2 + c)
    for dx, dy in offsets[:0:-1]:
        greet(expert_at(dx, dy, ps[0]), h)
    greet(e, 2 * (1 - zl) + c)
    greet(e, 2 * zl + 1 - c)
    for copy in loads[2:]:
        copy.start()

    loads[0].wait()
    loads[1].wait()
    tok[...] = tok4[...].reshape(rows_all, tok4.shape[2])
    logits = mm(tok[...], keys[...])
    folded = logits.reshape(rows_all // 8, 8, logits.shape[1])
    top = jnp.max(folded, axis=0)
    top = jnp.maximum(top, pltpu.roll(top, 4, 0))
    weight = jnp.exp(folded - top[None])
    total = jnp.sum(weight, axis=0)
    total = total + pltpu.roll(total, 4, 0)
    dispatch = (weight / total[None]).reshape(rows_all, logits.shape[1]).astype(BF)
    disp_all[...] = dispatch
    scores[...] = logits
    spread = onehot((128, 256), lambda r, q: q // 2 == r).astype(BF)
    image = lax.broadcasted_iota(jnp.int32, (rows_all, 256), 0) % 4
    wanted = c + 2 * (lax.broadcasted_iota(jnp.int32, (rows_all, 256), 1) % 2)

    def slots(scores, values):
        wide = jnp.where(image == wanted, mm(scores, spread), 0.0).astype(BF)
        return tn(wide, values).astype(BF).reshape(64, 2, 2, values.shape[1])

    def put(t, expert, hidden, slot, piece):
        return pltpu.make_async_remote_copy(
            src_ref=send.at[t, expert], dst_ref=rows[t].at[c, slot],
            send_sem=put_sem.at[t], recv_sem=got_sem.at[t, piece],
            device_id=(expert, hidden), device_id_type=MESH,
        )

    def send_all(t):
        def far(b):
            dx = b // 2
            expert = xs[dx] + swapped[2 * (b % 2) + dx % 2] + ps[2]
            put(t, expert, 2 * (1 - zl) + c, 16 + 8 * (1 - zl) + b, 0).start()

        def near(i):
            put(t, expert_at(*offsets[i], ahead), 2 * (1 - zl) + c, 32 * (1 - zl) + i, 1 + i // 4).start()

        def level(i):
            put(t, expert_at(*offsets[i], ps[0]), h, 48 + i, 5).start()

        pltpu.make_async_copy(send.at[t, e], rows[t].at[c, 48], self_sem.at[t]).start()
        for i in range(16):
            near(i)
            if t == 0 and 3 < i < 12:
                far(i - 4)
            if i:
                level((i + 7) % 15 + 1)
        if t == 1:
            for b in range(8):
                far(b)

    def wait_for(ref, sem):
        pltpu.make_async_copy(ref, ref, sem).wait()

    send[0] = slots(dispatch, tok[...])
    pl.semaphore_wait(barrier, 65)
    send_all(0)
    weight = jnp.exp(scores[...] - jnp.max(scores[...], axis=1, keepdims=True))
    comb_all[...] = (weight / jnp.sum(weight, axis=1, keepdims=True)).astype(BF)
    loads[2].wait()
    grad[...] = grad4[...].reshape(rows_all, grad4.shape[2])
    send[1] = slots(comb_all[...], grad[...])
    pair = (e, 2 * (1 - zl) + c)
    mate = (e, 2 * zl + 1 - c)
    starts = (
        16 + 8 * zl, *(32 * zl + 4 * q for q in range(4)), 48,
        16 + 8 * (1 - zl), *(32 * (1 - zl) + 4 * q for q in range(4)),
    )
    counts = (8, *(4,) * 4, 16, 8, *(4,) * 4)

    def piece_ref(t, i):
        return rows[t].at[c, pl.ds(starts[i], counts[i])]

    def share(t, i):
        pltpu.make_async_remote_copy(
            src_ref=piece_ref(t, i), dst_ref=piece_ref(t, i), send_sem=cput_sem.at[t, i],
            recv_sem=cgot_sem.at[t, i], device_id=mate, device_id_type=MESH,
        ).start()

    def forward(t, i):
        pltpu.make_async_remote_copy(
            src_ref=piece_ref(t, i), dst_ref=piece_ref(t, i), send_sem=fwd_sem.at[t, i],
            recv_sem=fgot_sem.at[t, i], device_id=pair, device_id_type=MESH,
        ).start()

    def take(t, i):
        if i == 5:
            wait_for(rows[t].at[c, pl.ds(49, 15)], got_sem.at[t, i])
            pltpu.make_async_copy(send.at[t, e], rows[t].at[c, 48], self_sem.at[t]).wait()
        elif i < 5:
            wait_for(piece_ref(t, i), got_sem.at[t, i])
            forward(t, i)
        else:
            wait_for(piece_ref(t, i), fgot_sem.at[t, i - 6])

    def complete(t):
        for i, count in enumerate(counts):
            wait_for(rows[t].at[c, pl.ds(0, count)], cgot_sem.at[t, i])

    width = tok4.shape[2]

    def gone(k):
        return (
            (pl.ds(16, 16), pl.ds(zl, 1)), (pl.ds(32 * (1 - zl) + 8, 8), pl.ds(0, 2)),
            (pl.ds(32 * (1 - zl), 8), pl.ds(0, 2)), (pl.ds(52, 12), pl.ds(1 - zl, 1)), (pl.ds(48, 4), pl.ds(1 - zl, 1)),
        )[k]

    def kept(k):
        return (
            (pl.ds(16, 16), pl.ds(1 - zl, 1)), (pl.ds(32 * zl + 8, 8), pl.ds(0, 2)),
            (pl.ds(32 * zl, 8), pl.ds(0, 2)), (pl.ds(52, 12), pl.ds(zl, 1)), (pl.ds(48, 4), pl.ds(zl, 1)),
        )[k]

    landing = (
        (pl.ds(16, 16), pl.ds(0, 1)), (pl.ds(8, 8), pl.ds(0, 2)),
        (pl.ds(0, 8), pl.ds(0, 2)), (pl.ds(20, 12), pl.ds(1, 1)), (pl.ds(16, 4), pl.ds(1, 1)),
    )

    def to_core(t):
        for half, pieces in enumerate((gone, kept)):
            for k in range(5):
                s, j = pieces(k)
                pltpu.make_async_remote_copy(
                    src_ref=part.at[t, 1 - c, s, j], dst_ref=fromcore.at[t, s, j], send_sem=rput_sem.at[t],
                    recv_sem=rgot_sem.at[t, half], device_id=mate, device_id_type=MESH,
                ).start()

    def add_core(t, half):
        wait_for(fromcore.at[t, pl.ds(0, 32)], rgot_sem.at[t, half])
        for k in range(5):
            s, j = (gone, kept)[half](k)
            part[t, c, s, j] = (part[t, c, s, j].astype(F32) + fromcore[t, s, j].astype(F32)).astype(BF)

    def to_pair(t, k):
        s, j = gone(k)
        ls, lj = landing[k]
        return pltpu.make_async_remote_copy(
            src_ref=part.at[t, c, s, j], dst_ref=frompair.at[t, ls, lj], send_sem=zput_sem.at[t, k],
            recv_sem=zgot_sem.at[t, k], device_id=pair, device_id_type=MESH,
        )

    def pair_up(t):
        add_core(t, 0)
        for k in range(5):
            to_pair(t, k).start()

    def add_pair(t, k):
        to_pair(t, k).wait_recv()
        s, j = kept(k)
        ls, lj = landing[k]
        frompair[t, ls, lj] = (frompair[t, ls, lj].astype(F32) + part[t, c, s, j].astype(F32)).astype(BF)

    def go_home(t, piece):
        def put_home(slot, j, expert, hidden):
            pltpu.make_async_remote_copy(
                src_ref=frompair.at[t, slot, j], dst_ref=home.at[t, e], send_sem=hput_sem.at[t],
                recv_sem=hgot_sem.at[t], device_id=(expert, hidden), device_id_type=MESH,
            ).start()

        def far():
            for par in (0, 1):
                for b, (dx, dy) in enumerate(checkered(par)):
                    put_home(16 + 8 * par + b, 0, expert_at(-dx, -dy, ps[2]), 2 * (1 - zl) + c)

        def near(first, last):
            for i in range(first, last):
                dx, dy = offsets[i]
                expert = expert_at(-dx, -dy, ahead)
                put_home(i, 0, expert, c)
                put_home(i, 1, expert, 2 + c)

        def level(first, last):
            for i in range(first, last):
                dx, dy = offsets[i]
                put_home(16 + i, 1, expert_at(-dx, -dy, ps[0]), h)

        add_pair(t, piece)
        if piece == 0:
            far()
        elif piece == 1:
            near(8, 16)
        elif piece == 2:
            near(0, 8)
        elif piece == 3:
            level(4, 16)
        else:
            pltpu.make_async_copy(frompair.at[t, 16, 1], home.at[t, e], hself_sem.at[t]).start()
            level(1, 4)

    def project(t, cc, weights):
        for k in range(2):
            rows_k = mm(act[k, pl.ds(pl.multiple_of(128 * cc, 128), 128)], weights[k])
            for n in range(width // 128):
                inter[n, pl.ds(k, 128, 2), :] = rows_k[:, 128 * n : 128 * n + 128]
        both = jnp.concatenate([inter[n] for n in range(width // 128)], axis=1)
        part[t, cc] = both.astype(BF).reshape(n_slots, 2, 2, width)


    def take_share(t, *pieces):
        for i in pieces:
            take(t, i)
            share(t, i)

    def take_on(t, *pieces):
        for i in pieces:
            take(t, i)

    def half_rows(t, k, cc):
        return rows[t][cc, :, k].reshape(128, width)

    def gate(k, cc):
        place = pl.ds(pl.multiple_of(128 * cc, 128), 128)
        pre = mm(half_rows(0, k, cc), win[k]) + bin_[k : k + 1]
        half = 0.5 * (1.0 + lax.erf(pre * 0.7071067811865476))
        slope[k, place] = half + pre * jnp.exp(-0.5 * pre * pre) * 0.3989422804014327
        act[k, place] = (pre * half).astype(BF)

    def slopes(cc):
        place = pl.ds(pl.multiple_of(128 * cc, 128), 128)
        for k in range(2):
            act[k, place] = (nt(half_rows(1, k, cc), wout[k]) * slope[k, place]).astype(BF)

    def slopes_all():
        for k in range(2):
            act[k] = (nt(rows[1][:, :, k].reshape(256, width), wout[k]) * slope[k]).astype(BF)

    def landed():
        for copy in loads[3:]:
            copy.wait()

    def flip():
        for k in range(2):
            flipped[k] = win[k].T

    landed()
    flip()
    take_share(0, 1)

    @pl.when(c == 0)
    def _():
        send_all(1)

    take_share(0, 2, 0, 3, 4, 5)

    @pl.when(c == 1)
    def _():
        send_all(1)

    take_share(0, 7, 8, 6, 9, 10)
    gate(0, c)
    gate(1, c)
    complete(0)
    take_on(1, 1, 2)
    gate(0, 1 - c)
    take_on(1, 3)
    gate(1, 1 - c)
    take_on(1, 4, 5)
    project(0, 1 - c, wout)
    to_core(0)
    take_on(1, 0)
    for piece in (1, 2, 3, 4, 5, 0):
        share(1, piece)
    project(0, c, wout)
    pair_up(0)
    take_share(1, 7, 8, 9, 10, 6)
    add_core(0, 1)
    complete(1)
    slopes_all()
    go_home(0, 0)
    project(1, 1 - c, flipped)
    to_core(1)
    go_home(0, 1)
    project(1, c, flipped)
    pair_up(1)
    for piece in range(2, 5):
        go_home(0, piece)
    add_core(1, 1)
    pick = onehot((positions, rows_all), lambda r, q: q == 4 * r + h).astype(BF)
    own_tok[...] = mm(pick, tok[...]).astype(BF)
    own_grad[...] = mm(pick, grad[...]).astype(BF)
    own_disp[...] = mm(pick, disp_all[...])
    own_comb[...] = mm(pick, comb_all[...])
    for piece in range(5):
        go_home(1, piece)

    def wait_home(t):
        wait_for(home.at[t, pl.ds(0, 63)], hgot_sem.at[t])
        pltpu.make_async_copy(frompair.at[t, 16, 1], home.at[t, e], hself_sem.at[t]).wait()

    wait_home(0)
    slot_out = (home[0].reshape(128, width).astype(F32) + bout[...]).astype(BF)
    comb = own_comb[...]
    disp = own_disp[...]
    comb_grad = nt(own_grad[...], slot_out)
    comb_term = comb * (comb_grad - jnp.sum(comb * comb_grad, axis=1, keepdims=True))
    wait_home(1)
    slot_in_grad = home[1].reshape(128, width)
    disp_grad = nt(own_tok[...], slot_in_grad)
    logit_grad = comb_term + disp * (disp_grad - jnp.sum(disp * disp_grad, axis=0, keepdims=True))
    result = mm(disp.astype(BF), slot_in_grad) + nt(logit_grad.astype(BF), keys[...])
    out_ref[...] = result.astype(BF)

    for t in range(2):
        wait_for(send.at[t, pl.ds(0, 39)], put_sem.at[t])
        for i in range(5):
            wait_for(rows[t].at[0, pl.ds(0, counts[i])], fwd_sem.at[t, i])
        for i, count in enumerate(counts):
            wait_for(rows[t].at[0, pl.ds(0, count)], cput_sem.at[t, i])
        wait_for(fromcore.at[t], rput_sem.at[t])
        for k in range(5):
            to_pair(t, k).wait_send()
        wait_for(home.at[t, pl.ds(0, 63)], hput_sem.at[t])


def local(tokens, slot_keys, w_in, b_in, w_out, b_out, out_grad):
    images, positions, width = tokens.shape
    units = w_in.shape[2]
    slots = slot_keys.shape[1]
    anyspec = pl.BlockSpec(memory_space=pl.ANY)
    dma = pltpu.SemaphoreType.DMA
    out = pl.pallas_call(
        kernel,
        out_shape=pltpu.VMEM((positions, width), BF),
        in_specs=[anyspec] * 7,
        out_specs=pl.BlockSpec(memory_space=pltpu.VMEM),
        scratch_shapes=[
            pltpu.VMEM((positions, images, width), BF),
            pltpu.VMEM((positions, images, width), BF),
            pltpu.VMEM((positions * images, width), BF),
            pltpu.VMEM((positions * images, width), BF),
            pltpu.VMEM((width, slots), BF),
            pltpu.VMEM((2, width, units), BF),
            pltpu.VMEM((2, units, width), BF),
            pltpu.VMEM((2, units), F32),
            pltpu.VMEM((slots, width), F32),
            pltpu.VMEM((2, 64, 2, 2, width), BF),
            pltpu.VMEM((2, 64, 2, 2, width), BF),
            pltpu.VMEM((2, 64, 2, 2, width), BF),
            pltpu.VMEM((2, 256, units), F32),
            pltpu.VMEM((2, 256, units), BF),
            pltpu.VMEM((width // 128, 256, 128), F32),
            pltpu.VMEM((2, 2, 64, 2, 2, width), BF),
            pltpu.VMEM((2, 64, 2, 2, width), BF),
            pltpu.VMEM((2, 32, 2, 2, width), BF),
            pltpu.VMEM((2, 64, 2, width), BF),
            pltpu.VMEM((positions, width), BF),
            pltpu.VMEM((positions, width), BF),
            pltpu.VMEM((positions, slots), F32),
            pltpu.VMEM((positions, slots), F32),
            pltpu.VMEM((positions * images, slots), BF),
            pltpu.VMEM((positions * images, slots), BF),
            pltpu.VMEM((positions * images, slots), F32),
            pltpu.VMEM((2, units, width), BF),
            dma((7,)), dma((2,)), dma((2, 6)), dma((2,)), dma((2, 5)), dma((2, 5)), dma((2, 11)), dma((2, 11)),
            dma((2,)), dma((2, 2)), dma((2, 5)), dma((2, 5)), dma((2,)), dma((2,)), dma((2,)),
        ],
        compiler_params=pltpu.CompilerParams(
            collective_id=0, has_side_effects=True, vmem_limit_bytes=58 * 1024 * 1024
        ),
        name="moe_input_grad",
    )(
        jnp.transpose(tokens, (1, 0, 2)), jnp.transpose(out_grad, (1, 0, 2)), slot_keys, w_in, b_in, w_out, b_out
    )
    return out[None]


def solution(mesh):
    return jax.shard_map(
        local,
        mesh=mesh,
        in_specs=(
            P("expert", None, None),
            P(),
            P("expert", None, "hidden"),
            P("expert", "hidden"),
            P("expert", "hidden", None),
            P(),
            P("expert", None, None),
        ),
        out_specs=P(("expert", "hidden"), None, None),
        check_vma=False,
    )
```

```python
import functools

import jax
import jax.numpy as jnp
from jax import lax
from jax.experimental import pallas as pl
from jax.experimental.pallas import tpu as pltpu
from jax.sharding import PartitionSpec as P

BF = jnp.bfloat16
F32 = jnp.float32
MESH = pl.DeviceIdType.MESH
NT = (((1,), (1,)), ((), ()))
TN = (((0,), (0,)), ((), ()))


def mm(a, b):
    return jnp.dot(a, b, preferred_element_type=F32)


def nt(a, b):
    return lax.dot_general(a, b, NT, preferred_element_type=F32)


def tn(a, b):
    return lax.dot_general(a, b, TN, preferred_element_type=F32)


def onehot(shape, test):
    rows = lax.broadcasted_iota(jnp.int32, shape, 0)
    cols = lax.broadcasted_iota(jnp.int32, shape, 1)
    return jnp.where(test(rows, cols), 1.0, 0.0)


def kernel(
    tok_h, grad_h, keys_h, win_h, bin_h, wout_h, bout_h,
    out_ref,
    tok4, grad4, tok, grad, keys, win, wout, bin_, bout,
    send, rows0, rows1, slope, act, inter, part, fromcore, frompair, home,
    own_tok, own_grad, own_disp, own_comb, comb_all, disp_all, scores, flipped, flipped_out,
    load_sem, put_sem, got_sem, self_sem, fwd_sem, fgot_sem, cput_sem, cgot_sem,
    rput_sem, rgot_sem, zput_sem, zgot_sem, hput_sem, hgot_sem, hself_sem,
):
    e = lax.axis_index("expert")
    h = lax.axis_index("hidden")
    x, y, p = e // 16, (e // 4) % 4, e % 4
    zl, c = h // 2, h % 2
    n_slots, positions = 64, tok4.shape[0]
    rows_all = positions * 4
    rows = (rows0, rows1)

    xs = [lax.rem(x + d, 4) * 16 for d in range(4)]
    ys = [lax.rem(y + d, 4) * 4 for d in range(4)]
    ps = [lax.rem(p + d, 4) for d in range(4)]
    ahead = lax.rem(p + 3 - 2 * zl, 4)
    offsets = (
        (0, 0), (1, 0), (0, 1), (3, 0), (0, 3), (1, 1), (3, 3), (1, 3),
        (3, 1), (2, 0), (0, 2), (2, 1), (1, 2), (2, 3), (3, 2), (2, 2),
    )

    def expert_at(dx, dy, plane):
        return xs[dx % 4] + ys[dy % 4] + plane

    def checkered(flip):
        return [(b // 2, 2 * (b % 2) + (b // 2 + flip) % 2) for b in range(8)]

    swapped = [lax.rem(y + d, 4) * 4 for d in (1 - zl, zl, 3 - zl, 2 + zl)]

    loads = [
        pltpu.make_async_copy(src, dst, load_sem.at[i])
        for i, (src, dst) in enumerate((
            (tok_h, tok4), (keys_h, keys), (grad_h, grad4), (win_h, win), (bin_h, bin_),
            (wout_h, wout), (bout_h, bout),
        ))
    ]
    loads[0].start()
    loads[1].start()

    barrier = pltpu.get_barrier_semaphore()

    def greet(expert, hidden):
        pl.semaphore_signal(barrier, inc=1, device_id=(expert, hidden), device_id_type=MESH)

    for dx, dy in offsets[::-1]:
        greet(expert_at(dx, dy, ps[2]), 2 * (1 - zl) + c)
        greet(expert_at(dx, dy, ps[1]), c)
        greet(expert_at(dx, dy, ps[3]), 2 + c)
    for dx, dy in offsets[:0:-1]:
        greet(expert_at(dx, dy, ps[0]), h)
    greet(e, 2 * (1 - zl) + c)
    greet(e, 2 * zl + 1 - c)
    for copy in loads[2:]:
        copy.start()

    loads[0].wait()
    loads[1].wait()
    tok[...] = tok4[...].reshape(rows_all, tok4.shape[2])
    logits = mm(tok[...], keys[...])
    folded = logits.reshape(rows_all // 8, 8, logits.shape[1])
    top = jnp.max(folded, axis=0)
    top = jnp.maximum(top, pltpu.roll(top, 4, 0))
    weight = jnp.exp(folded - top[None])
    total = jnp.sum(weight, axis=0)
    total = total + pltpu.roll(total, 4, 0)
    dispatch = (weight / total[None]).reshape(rows_all, logits.shape[1]).astype(BF)
    disp_all[...] = dispatch
    scores[...] = logits
    spread = onehot((128, 256), lambda r, q: q // 2 == r).astype(BF)
    image = lax.broadcasted_iota(jnp.int32, (rows_all, 256), 0) % 4
    wanted = c + 2 * (lax.broadcasted_iota(jnp.int32, (rows_all, 256), 1) % 2)

    def slots(scores, values):
        wide = jnp.where(image == wanted, mm(scores, spread), 0.0).astype(BF)
        return tn(wide, values).astype(BF).reshape(64, 2, 2, values.shape[1])

    def put(t, expert, hidden, slot, piece):
        return pltpu.make_async_remote_copy(
            src_ref=send.at[t, expert], dst_ref=rows[t].at[c, slot],
            send_sem=put_sem.at[t], recv_sem=got_sem.at[t, piece],
            device_id=(expert, hidden), device_id_type=MESH,
        )

    def send_near(t):
        for i in range(16):
            expert = expert_at(*offsets[i], ahead)
            put(t, expert, 2 * (1 - zl) + c, 16 * (1 - zl) + i, i // 8).start()

    def send_rest(t):
        pltpu.make_async_copy(send.at[t, e], rows[t].at[c, 48], self_sem.at[t]).start()
        for i in range(1, 16):
            if i <= 8:
                b = i - 1
                expert = xs[b // 2] + swapped[2 * (b % 2) + (b // 2) % 2] + ps[2]
                put(t, expert, 2 * (1 - zl) + c, 32 + 8 * (1 - zl) + b, 2).start()
            put(t, expert_at(*offsets[i], ps[0]), h, 48 + i, 3).start()

    def wait_for(ref, sem):
        pltpu.make_async_copy(ref, ref, sem).wait()

    send[0] = slots(dispatch, tok[...])
    pl.semaphore_wait(barrier, 65)
    send_near(0)
    weight = jnp.exp(scores[...] - jnp.max(scores[...], axis=1, keepdims=True))
    comb_all[...] = (weight / jnp.sum(weight, axis=1, keepdims=True)).astype(BF)
    loads[2].wait()
    grad[...] = grad4[...].reshape(rows_all, grad4.shape[2])
    send[1] = slots(comb_all[...], grad[...])
    pair = (e, 2 * (1 - zl) + c)
    mate = (e, 2 * zl + 1 - c)
    starts = (
        16 * zl, 16 * zl + 8, 32 + 8 * zl, 48, 16 * (1 - zl), 16 * (1 - zl) + 8, 32 + 8 * (1 - zl),
    )
    counts = (8, 8, 8, 16, 8, 8, 8)

    def piece_ref(t, i):
        return rows[t].at[c, pl.ds(starts[i], counts[i])]

    def share(t, i):
        pltpu.make_async_remote_copy(
            src_ref=piece_ref(t, i), dst_ref=piece_ref(t, i), send_sem=cput_sem.at[t],
            recv_sem=cgot_sem.at[t, int(i in (2, 3, 6))], device_id=mate, device_id_type=MESH,
        ).start()

    def forward(t, i):
        pltpu.make_async_remote_copy(
            src_ref=piece_ref(t, i), dst_ref=piece_ref(t, i), send_sem=fwd_sem.at[t],
            recv_sem=fgot_sem.at[t, i], device_id=pair, device_id_type=MESH,
        ).start()

    def take(t, *pieces):
        for i in pieces:
            if i == 3:
                wait_for(rows[t].at[c, pl.ds(49, 15)], got_sem.at[t, i])
                pltpu.make_async_copy(send.at[t, e], rows[t].at[c, 48], self_sem.at[t]).wait()
            elif i < 3:
                wait_for(piece_ref(t, i), got_sem.at[t, i])
                forward(t, i)
            else:
                wait_for(piece_ref(t, i), fgot_sem.at[t, i - 4])

    def share_all(t, *pieces):
        for i in pieces:
            share(t, i)

    def complete(t, part_of):
        wait_for(rows[t].at[c, pl.ds(0, 32)], cgot_sem.at[t, part_of])

    width = tok4.shape[2]

    def gone(k):
        return (
            (pl.ds(16 * (1 - zl) + 8, 8), pl.ds(0, 2)), (pl.ds(16 * (1 - zl), 8), pl.ds(0, 2)),
            (pl.ds(32, 16), pl.ds(zl, 1)), (pl.ds(52, 12), pl.ds(1 - zl, 1)), (pl.ds(48, 4), pl.ds(1 - zl, 1)),
        )[k]

    def kept(k):
        return (
            (pl.ds(16 * zl + 8, 8), pl.ds(0, 2)), (pl.ds(16 * zl, 8), pl.ds(0, 2)),
            (pl.ds(32, 16), pl.ds(1 - zl, 1)), (pl.ds(52, 12), pl.ds(zl, 1)), (pl.ds(48, 4), pl.ds(zl, 1)),
        )[k]

    landing = (
        (pl.ds(8, 8), pl.ds(0, 2)), (pl.ds(0, 8), pl.ds(0, 2)),
        (pl.ds(16, 16), pl.ds(0, 1)), (pl.ds(20, 12), pl.ds(1, 1)), (pl.ds(16, 4), pl.ds(1, 1)),
    )
    members = ((0, 1), (2, 3, 4))

    def to_core(t, u):
        for half, pieces in enumerate((gone, kept)):
            for k in members[u]:
                s, j = pieces(k)
                pltpu.make_async_remote_copy(
                    src_ref=part.at[t, 1 - c, s, j], dst_ref=fromcore.at[t, s, j], send_sem=rput_sem.at[t],
                    recv_sem=rgot_sem.at[t, 2 * u + half], device_id=mate, device_id_type=MESH,
                ).start()

    def add_core(t, u, half):
        wait_for(fromcore.at[t, pl.ds(0, 16)], rgot_sem.at[t, 2 * u + half])
        for k in members[u]:
            s, j = (gone, kept)[half](k)
            part[t, c, s, j] = (part[t, c, s, j].astype(F32) + fromcore[t, s, j].astype(F32)).astype(BF)

    def to_pair(t, k):
        s, j = gone(k)
        ls, lj = landing[k]
        return pltpu.make_async_remote_copy(
            src_ref=part.at[t, c, s, j], dst_ref=frompair.at[t, ls, lj], send_sem=zput_sem.at[t],
            recv_sem=zgot_sem.at[t, k], device_id=pair, device_id_type=MESH,
        )

    def queue(*pieces):
        for t, k in pieces:
            to_pair(t, k).start()

    def pair_up(t, u, *more):
        add_core(t, u, 0)
        for tt, k in more or [(t, k) for k in members[u]]:
            to_pair(tt, k).start()

    def add_pair(t, k):
        to_pair(t, k).wait_recv()
        s, j = kept(k)
        ls, lj = landing[k]
        frompair[t, ls, lj] = (frompair[t, ls, lj].astype(F32) + part[t, c, s, j].astype(F32)).astype(BF)

    def go_home(t, piece):
        def put_home(slot, j, expert, hidden):
            pltpu.make_async_remote_copy(
                src_ref=frompair.at[t, slot, j], dst_ref=home.at[t, e], send_sem=hput_sem.at[t],
                recv_sem=hgot_sem.at[t], device_id=(expert, hidden), device_id_type=MESH,
            ).start()

        def far():
            for par in (0, 1):
                for b, (dx, dy) in enumerate(checkered(par)):
                    put_home(16 + 8 * par + b, 0, expert_at(-dx, -dy, ps[2]), 2 * (1 - zl) + c)

        def near(first, last):
            for i in range(first, last):
                dx, dy = offsets[i]
                expert = expert_at(-dx, -dy, ahead)
                put_home(i, 0, expert, c)
                put_home(i, 1, expert, 2 + c)

        def level(first, last):
            for i in range(first, last):
                dx, dy = offsets[i]
                put_home(16 + i, 1, expert_at(-dx, -dy, ps[0]), h)

        add_pair(t, piece)
        if piece == 0:
            near(8, 16)
        elif piece == 1:
            near(0, 8)
        elif piece == 2:
            far()
        elif piece == 3:
            level(4, 16)
        else:
            pltpu.make_async_copy(frompair.at[t, 16, 1], home.at[t, e], hself_sem.at[t]).start()
            level(1, 4)

    def unit_rows(t, k, u):
        return rows[t][:, 32 * u : 32 * u + 32, k].reshape(128, width)

    def gate(u):
        for k in range(2):
            pre = mm(unit_rows(0, k, u), win[k]) + bin_[k : k + 1]
            half = 0.5 * (1.0 + lax.erf(pre * 0.7071067811865476))
            slope[k] = half + pre * jnp.exp(-0.5 * pre * pre) * 0.3989422804014327
            act[k] = (pre * half).astype(BF)

    def slopes(u):
        for k in range(2):
            act[k] = (mm(unit_rows(1, k, u), flipped_out[k]) * slope[k]).astype(BF)

    def project(t, u, weights):
        for k in range(2):
            rows_k = mm(act[k], weights[k])
            for n in range(width // 128):
                inter[n, pl.ds(k, 128, 2), :] = rows_k[:, 128 * n : 128 * n + 128]
        both = jnp.concatenate([inter[n] for n in range(width // 128)], axis=1)
        part[t, :, 32 * u : 32 * u + 32] = both.astype(BF).reshape(2, 32, 2, 2, width)
        to_core(t, u)

    def own_image():
        pick = onehot((positions, rows_all), lambda r, q: q == 4 * r + h).astype(BF)
        own_tok[...] = mm(pick, tok[...]).astype(BF)
        own_grad[...] = mm(pick, grad[...]).astype(BF)
        own_disp[...] = mm(pick, disp_all[...])
        own_comb[...] = mm(pick, comb_all[...])
    def landed():
        for copy in loads[3:]:
            copy.wait()

    def flip(k):
        flipped[k] = win[k].T
        flipped_out[k] = wout[k].T

    send_near(1)
    send_rest(0)
    landed()
    flip(0)
    take(0, 0)
    share_all(0, 0)
    flip(1)
    take(0, 1)
    share_all(0, 1)
    take(1, 0)
    send_rest(1)
    own_image()
    take(1, 1)
    take(0, 4, 5)
    share_all(0, 4, 5)
    take(0, 2)
    complete(0, 0)
    gate(0)
    share_all(1, 0, 1)
    take(1, 4)
    share_all(1, 4)
    project(0, 0, wout)
    take(1, 5)
    share_all(1, 5)
    take(0, 3)
    share_all(0, 2, 3)
    pair_up(0, 0)
    add_core(0, 0, 1)
    complete(1, 0)
    slopes(0)
    take(1, 2)
    project(1, 0, flipped)
    take(0, 6)
    share_all(0, 6)
    take(1, 3)
    share_all(1, 2, 3)
    pair_up(1, 0)
    add_core(1, 0, 1)
    complete(0, 1)
    gate(1)
    take(1, 6)
    share_all(1, 6)
    project(0, 1, wout)
    go_home(0, 0)
    go_home(0, 1)
    pair_up(0, 1, (0, 2))
    add_core(0, 1, 1)
    complete(1, 1)
    slopes(1)
    project(1, 1, flipped)
    go_home(1, 0)
    go_home(1, 1)
    pair_up(1, 1, (1, 2), (0, 3), (1, 3), (0, 4), (1, 4))
    add_core(1, 1, 1)
    for piece in (2, 3, 4):
        go_home(0, piece)
        go_home(1, piece)

    def wait_home(t):
        wait_for(home.at[t, pl.ds(0, 63)], hgot_sem.at[t])
        pltpu.make_async_copy(frompair.at[t, 16, 1], home.at[t, e], hself_sem.at[t]).wait()

    wait_home(0)
    slot_out = (home[0].reshape(128, width).astype(F32) + bout[...]).astype(BF)
    comb = own_comb[...]
    disp = own_disp[...]
    comb_grad = nt(own_grad[...], slot_out)
    comb_term = comb * (comb_grad - jnp.sum(comb * comb_grad, axis=1, keepdims=True))
    wait_home(1)
    slot_in_grad = home[1].reshape(128, width)
    disp_grad = nt(own_tok[...], slot_in_grad)
    logit_grad = comb_term + disp * (disp_grad - jnp.sum(disp * disp_grad, axis=0, keepdims=True))
    result = mm(disp.astype(BF), slot_in_grad) + nt(logit_grad.astype(BF), keys[...])
    out_ref[...] = result.astype(BF)

    for t in range(2):
        wait_for(send.at[t, pl.ds(0, 39)], put_sem.at[t])
        wait_for(rows[t].at[0, pl.ds(0, 24)], fwd_sem.at[t])
        wait_for(rows[t].at[0], cput_sem.at[t])
        wait_for(fromcore.at[t], rput_sem.at[t])
        wait_for(frompair.at[t], zput_sem.at[t])
        wait_for(home.at[t, pl.ds(0, 63)], hput_sem.at[t])


def local(tokens, slot_keys, w_in, b_in, w_out, b_out, out_grad):
    images, positions, width = tokens.shape
    units = w_in.shape[2]
    slots = slot_keys.shape[1]
    anyspec = pl.BlockSpec(memory_space=pl.ANY)
    dma = pltpu.SemaphoreType.DMA
    out = pl.pallas_call(
        kernel,
        out_shape=pltpu.VMEM((positions, width), BF),
        in_specs=[anyspec] * 7,
        out_specs=pl.BlockSpec(memory_space=pltpu.VMEM),
        scratch_shapes=[
            pltpu.VMEM((positions, images, width), BF),
            pltpu.VMEM((positions, images, width), BF),
            pltpu.VMEM((positions * images, width), BF),
            pltpu.VMEM((positions * images, width), BF),
            pltpu.VMEM((width, slots), BF),
            pltpu.VMEM((2, width, units), BF),
            pltpu.VMEM((2, units, width), BF),
            pltpu.VMEM((2, units), F32),
            pltpu.VMEM((slots, width), F32),
            pltpu.VMEM((2, 64, 2, 2, width), BF),
            pltpu.VMEM((2, 64, 2, 2, width), BF),
            pltpu.VMEM((2, 64, 2, 2, width), BF),
            pltpu.VMEM((2, 128, units), F32),
            pltpu.VMEM((2, 128, units), BF),
            pltpu.VMEM((width // 128, 256, 128), F32),
            pltpu.VMEM((2, 2, 64, 2, 2, width), BF),
            pltpu.VMEM((2, 64, 2, 2, width), BF),
            pltpu.VMEM((2, 32, 2, 2, width), BF),
            pltpu.VMEM((2, 64, 2, width), BF),
            pltpu.VMEM((positions, width), BF),
            pltpu.VMEM((positions, width), BF),
            pltpu.VMEM((positions, slots), F32),
            pltpu.VMEM((positions, slots), F32),
            pltpu.VMEM((positions * images, slots), BF),
            pltpu.VMEM((positions * images, slots), BF),
            pltpu.VMEM((positions * images, slots), F32),
            pltpu.VMEM((2, units, width), BF),
            pltpu.VMEM((2, width, units), BF),
            dma((7,)), dma((2,)), dma((2, 4)), dma((2,)), dma((2,)), dma((2, 3)), dma((2,)), dma((2, 2)),
            dma((2,)), dma((2, 4)), dma((2,)), dma((2, 5)), dma((2,)), dma((2,)), dma((2,)),
        ],
        compiler_params=pltpu.CompilerParams(
            collective_id=0, has_side_effects=True, vmem_limit_bytes=58 * 1024 * 1024
        ),
        name="moe_input_grad",
    )(
        jnp.transpose(tokens, (1, 0, 2)), jnp.transpose(out_grad, (1, 0, 2)), slot_keys, w_in, b_in, w_out, b_out
    )
    return out[None]


def solution(mesh):
    return jax.shard_map(
        local,
        mesh=mesh,
        in_specs=(
            P("expert", None, None),
            P(),
            P("expert", None, "hidden"),
            P("expert", "hidden"),
            P("expert", "hidden", None),
            P(),
            P("expert", None, None),
        ),
        out_specs=P(("expert", "hidden"), None, None),
        check_vma=False,
    )
```

```python
import functools

import jax
import jax.numpy as jnp
from jax import lax
from jax.experimental import pallas as pl
from jax.experimental.pallas import tpu as pltpu
from jax.sharding import PartitionSpec as P

BF = jnp.bfloat16
F32 = jnp.float32
MESH = pl.DeviceIdType.MESH
NT = (((1,), (1,)), ((), ()))
TN = (((0,), (0,)), ((), ()))


def mm(a, b):
    return jnp.dot(a, b, preferred_element_type=F32)


def nt(a, b):
    return lax.dot_general(a, b, NT, preferred_element_type=F32)


def tn(a, b):
    return lax.dot_general(a, b, TN, preferred_element_type=F32)


def onehot(shape, test):
    rows = lax.broadcasted_iota(jnp.int32, shape, 0)
    cols = lax.broadcasted_iota(jnp.int32, shape, 1)
    return jnp.where(test(rows, cols), 1.0, 0.0)


def kernel(
    tok_h, grad_h, keys_h, win_h, bin_h, wout_h, bout_h,
    out_ref,
    tok4, grad4, tok, grad, keys, win, wout, bin_, bout,
    send, rows0, rows1, slope, act, inter, part, fromcore, frompair, home,
    own_tok, own_grad, own_disp, own_comb, comb_all, disp_all, scores, flipped, flipped_out,
    load_sem, put_sem, got_sem, self_sem, fwd_sem, fgot_sem, cput_sem, cgot_sem,
    rput_sem, rgot_sem, zput_sem, zgot_sem, hput_sem, hgot_sem, hself_sem,
):
    e = lax.axis_index("expert")
    h = lax.axis_index("hidden")
    x, y, p = e // 16, (e // 4) % 4, e % 4
    zl, c = h // 2, h % 2
    n_slots, positions = 64, tok4.shape[0]
    rows_all = positions * 4
    rows = (rows0, rows1)

    xs = [lax.rem(x + d, 4) * 16 for d in range(4)]
    ys = [lax.rem(y + d, 4) * 4 for d in range(4)]
    ps = [lax.rem(p + d, 4) for d in range(4)]
    ahead = lax.rem(p + 3 - 2 * zl, 4)
    offsets = (
        (0, 0), (1, 0), (0, 1), (3, 0), (0, 3), (1, 1), (3, 3), (1, 3),
        (3, 1), (2, 0), (0, 2), (2, 1), (1, 2), (2, 3), (3, 2), (2, 2),
    )

    def expert_at(dx, dy, plane):
        return xs[dx % 4] + ys[dy % 4] + plane

    def checkered(flip):
        return [(b // 2, 2 * (b % 2) + (b // 2 + flip) % 2) for b in range(8)]

    swapped = [lax.rem(y + d, 4) * 4 for d in (1 - zl, zl, 3 - zl, 2 + zl)]

    loads = [
        pltpu.make_async_copy(src, dst, load_sem.at[i])
        for i, (src, dst) in enumerate((
            (tok_h, tok4), (keys_h, keys), (grad_h, grad4), (win_h, win), (bin_h, bin_),
            (wout_h, wout), (bout_h, bout),
        ))
    ]
    loads[0].start()
    loads[1].start()

    barrier = pltpu.get_barrier_semaphore()

    def greet(expert, hidden):
        pl.semaphore_signal(barrier, inc=1, device_id=(expert, hidden), device_id_type=MESH)

    for dx, dy in offsets[::-1]:
        greet(expert_at(dx, dy, ps[2]), 2 * (1 - zl) + c)
        greet(expert_at(dx, dy, ps[1]), c)
        greet(expert_at(dx, dy, ps[3]), 2 + c)
    for dx, dy in offsets[:0:-1]:
        greet(expert_at(dx, dy, ps[0]), h)
    greet(e, 2 * (1 - zl) + c)
    greet(e, 2 * zl + 1 - c)
    for copy in loads[2:]:
        copy.start()

    loads[0].wait()
    loads[1].wait()
    tok[...] = tok4[...].reshape(rows_all, tok4.shape[2])
    logits = mm(tok[...], keys[...])
    folded = logits.reshape(rows_all // 8, 8, logits.shape[1])
    top = jnp.max(folded, axis=0)
    top = jnp.maximum(top, pltpu.roll(top, 4, 0))
    weight = jnp.exp(folded - top[None])
    total = jnp.sum(weight, axis=0)
    total = total + pltpu.roll(total, 4, 0)
    dispatch = (weight / total[None]).reshape(rows_all, logits.shape[1]).astype(BF)
    disp_all[...] = dispatch
    scores[...] = logits
    spread = onehot((128, 256), lambda r, q: q // 2 == r).astype(BF)
    image = lax.broadcasted_iota(jnp.int32, (rows_all, 256), 0) % 4
    wanted = c + 2 * (lax.broadcasted_iota(jnp.int32, (rows_all, 256), 1) % 2)

    def slots(scores, values):
        wide = jnp.where(image == wanted, mm(scores, spread), 0.0).astype(BF)
        return tn(wide, values).astype(BF).reshape(64, 2, 2, values.shape[1])

    def put(t, expert, hidden, slot, piece):
        return pltpu.make_async_remote_copy(
            src_ref=send.at[t, expert], dst_ref=rows[t].at[c, slot],
            send_sem=put_sem.at[t], recv_sem=got_sem.at[t, piece],
            device_id=(expert, hidden), device_id_type=MESH,
        )

    def send_near(t):
        for i in range(16):
            expert = expert_at(*offsets[i], ahead)
            put(t, expert, 2 * (1 - zl) + c, 16 * (1 - zl) + i, i // 8).start()

    def send_rest(t):
        pltpu.make_async_copy(send.at[t, e], rows[t].at[c, 48], self_sem.at[t]).start()
        for i in range(1, 16):
            if i <= 8:
                b = i - 1
                expert = xs[b // 2] + swapped[2 * (b % 2) + (b // 2) % 2] + ps[2]
                put(t, expert, 2 * (1 - zl) + c, 32 + 8 * (1 - zl) + b, 2).start()
            put(t, expert_at(*offsets[i], ps[0]), h, 48 + i, 3).start()

    def wait_for(ref, sem):
        pltpu.make_async_copy(ref, ref, sem).wait()

    send[0] = slots(dispatch, tok[...])
    pl.semaphore_wait(barrier, 65)
    send_near(0)
    weight = jnp.exp(scores[...] - jnp.max(scores[...], axis=1, keepdims=True))
    comb_all[...] = (weight / jnp.sum(weight, axis=1, keepdims=True)).astype(BF)
    loads[2].wait()
    grad[...] = grad4[...].reshape(rows_all, grad4.shape[2])
    send[1] = slots(comb_all[...], grad[...])
    pair = (e, 2 * (1 - zl) + c)
    mate = (e, 2 * zl + 1 - c)
    starts = (
        16 * zl, 16 * zl + 8, 32 + 8 * zl, 48, 16 * (1 - zl), 16 * (1 - zl) + 8, 32 + 8 * (1 - zl),
    )
    counts = (8, 8, 8, 16, 8, 8, 8)

    def piece_ref(t, i):
        return rows[t].at[c, pl.ds(starts[i], counts[i])]

    def share(t, i):
        pltpu.make_async_remote_copy(
            src_ref=piece_ref(t, i), dst_ref=piece_ref(t, i), send_sem=cput_sem.at[t],
            recv_sem=cgot_sem.at[t, int(i in (2, 3, 6))], device_id=mate, device_id_type=MESH,
        ).start()

    def forward(t, i):
        pltpu.make_async_remote_copy(
            src_ref=piece_ref(t, i), dst_ref=piece_ref(t, i), send_sem=fwd_sem.at[t],
            recv_sem=fgot_sem.at[t, i], device_id=pair, device_id_type=MESH,
        ).start()

    def take(t, *pieces):
        for i in pieces:
            if i == 3:
                wait_for(rows[t].at[c, pl.ds(49, 15)], got_sem.at[t, i])
                pltpu.make_async_copy(send.at[t, e], rows[t].at[c, 48], self_sem.at[t]).wait()
            elif i < 3:
                wait_for(piece_ref(t, i), got_sem.at[t, i])
                forward(t, i)
            else:
                wait_for(piece_ref(t, i), fgot_sem.at[t, i - 4])

    def share_all(t, *pieces):
        for i in pieces:
            share(t, i)

    def complete(t, part_of):
        wait_for(rows[t].at[c, pl.ds(0, 32)], cgot_sem.at[t, part_of])

    width = tok4.shape[2]

    def gone(k):
        return (
            (pl.ds(16 * (1 - zl) + 8, 8), pl.ds(0, 2)), (pl.ds(16 * (1 - zl), 8), pl.ds(0, 2)),
            (pl.ds(32, 16), pl.ds(zl, 1)), (pl.ds(52, 12), pl.ds(1 - zl, 1)), (pl.ds(48, 4), pl.ds(1 - zl, 1)),
        )[k]

    def kept(k):
        return (
            (pl.ds(16 * zl + 8, 8), pl.ds(0, 2)), (pl.ds(16 * zl, 8), pl.ds(0, 2)),
            (pl.ds(32, 16), pl.ds(1 - zl, 1)), (pl.ds(52, 12), pl.ds(zl, 1)), (pl.ds(48, 4), pl.ds(zl, 1)),
        )[k]

    landing = (
        (pl.ds(8, 8), pl.ds(0, 2)), (pl.ds(0, 8), pl.ds(0, 2)),
        (pl.ds(16, 16), pl.ds(0, 1)), (pl.ds(20, 12), pl.ds(1, 1)), (pl.ds(16, 4), pl.ds(1, 1)),
    )
    members = ((0, 1), (2, 3, 4))

    def to_core(t, u):
        for half, pieces in enumerate((gone, kept)):
            for k in members[u]:
                s, j = pieces(k)
                pltpu.make_async_remote_copy(
                    src_ref=part.at[t, 1 - c, s, j], dst_ref=fromcore.at[t, s, j], send_sem=rput_sem.at[t],
                    recv_sem=rgot_sem.at[t, 2 * u + half], device_id=mate, device_id_type=MESH,
                ).start()

    def add_core(t, u, half):
        wait_for(fromcore.at[t, pl.ds(0, 16)], rgot_sem.at[t, 2 * u + half])
        for k in members[u]:
            s, j = (gone, kept)[half](k)
            part[t, c, s, j] = (part[t, c, s, j].astype(F32) + fromcore[t, s, j].astype(F32)).astype(BF)

    def to_pair(t, k):
        s, j = gone(k)
        ls, lj = landing[k]
        return pltpu.make_async_remote_copy(
            src_ref=part.at[t, c, s, j], dst_ref=frompair.at[t, ls, lj], send_sem=zput_sem.at[t],
            recv_sem=zgot_sem.at[t, k], device_id=pair, device_id_type=MESH,
        )

    def pair_up(t, u, *more):
        add_core(t, u, 0)
        for tt, k in more or [(t, k) for k in members[u]]:
            to_pair(tt, k).start()

    def add_pair(t, k):
        to_pair(t, k).wait_recv()
        s, j = kept(k)
        ls, lj = landing[k]
        frompair[t, ls, lj] = (frompair[t, ls, lj].astype(F32) + part[t, c, s, j].astype(F32)).astype(BF)

    def go_home(t, piece):
        def put_home(slot, j, expert, hidden):
            pltpu.make_async_remote_copy(
                src_ref=frompair.at[t, slot, j], dst_ref=home.at[t, e], send_sem=hput_sem.at[t],
                recv_sem=hgot_sem.at[t], device_id=(expert, hidden), device_id_type=MESH,
            ).start()

        def far():
            for par in (0, 1):
                for b, (dx, dy) in enumerate(checkered(par)):
                    put_home(16 + 8 * par + b, 0, expert_at(-dx, -dy, ps[2]), 2 * (1 - zl) + c)

        def near(first, last):
            for i in range(first, last):
                dx, dy = offsets[i]
                expert = expert_at(-dx, -dy, ahead)
                put_home(i, 0, expert, c)
                put_home(i, 1, expert, 2 + c)

        def level(first, last):
            for i in range(first, last):
                dx, dy = offsets[i]
                put_home(16 + i, 1, expert_at(-dx, -dy, ps[0]), h)

        add_pair(t, piece)
        if piece == 0:
            near(8, 16)
        elif piece == 1:
            near(0, 8)
        elif piece == 2:
            far()
        elif piece == 3:
            level(4, 16)
        else:
            pltpu.make_async_copy(frompair.at[t, 16, 1], home.at[t, e], hself_sem.at[t]).start()
            level(1, 4)

    def unit_rows(t, k, u):
        return rows[t][:, 32 * u : 32 * u + 32, k].reshape(128, width)

    def gate(u):
        for k in range(2):
            pre = mm(unit_rows(0, k, u), win[k]) + bin_[k : k + 1]
            half = 0.5 * (1.0 + lax.erf(pre * 0.7071067811865476))
            slope[k] = half + pre * jnp.exp(-0.5 * pre * pre) * 0.3989422804014327
            act[k] = (pre * half).astype(BF)

    def slopes(u):
        for k in range(2):
            act[k] = (mm(unit_rows(1, k, u), flipped_out[k]) * slope[k]).astype(BF)

    def project(t, u, weights):
        for k in range(2):
            rows_k = mm(act[k], weights[k])
            for n in range(width // 128):
                inter[n, pl.ds(k, 128, 2), :] = rows_k[:, 128 * n : 128 * n + 128]
        both = jnp.concatenate([inter[n] for n in range(width // 128)], axis=1)
        part[t, :, 32 * u : 32 * u + 32] = both.astype(BF).reshape(2, 32, 2, 2, width)
        to_core(t, u)

    def own_image():
        pick = onehot((positions, rows_all), lambda r, q: q == 4 * r + h).astype(BF)
        own_tok[...] = mm(pick, tok[...]).astype(BF)
        own_grad[...] = mm(pick, grad[...]).astype(BF)
        own_disp[...] = mm(pick, disp_all[...])
        own_comb[...] = mm(pick, comb_all[...])
    def landed():
        for copy in loads[3:]:
            copy.wait()

    def flip(k):
        flipped[k] = win[k].T
        flipped_out[k] = wout[k].T

    send_near(1)
    send_rest(0)
    landed()
    flip(0)
    take(0, 0)
    share_all(0, 0)
    flip(1)
    take(0, 1)
    share_all(0, 1)
    take(1, 0)
    send_rest(1)
    own_image()
    take(1, 1)
    take(0, 4, 5)
    share_all(0, 4, 5)
    take(0, 2)
    complete(0, 0)
    gate(0)
    share_all(1, 0, 1)
    take(1, 4)
    share_all(1, 4)
    project(0, 0, wout)
    take(1, 5)
    share_all(1, 5)
    take(0, 3)
    share_all(0, 2, 3)
    take(1, 2)
    pair_up(0, 0)
    add_core(0, 0, 1)
    complete(1, 0)
    slopes(0)
    project(1, 0, flipped)
    take(0, 6)
    share_all(0, 6)
    take(1, 3)
    share_all(1, 2, 3)
    pair_up(1, 0)
    add_core(1, 0, 1)
    complete(0, 1)
    gate(1)
    take(1, 6)
    share_all(1, 6)
    project(0, 1, wout)
    go_home(0, 0)
    pair_up(0, 1, (0, 2))
    go_home(0, 1)
    add_core(0, 1, 1)
    complete(1, 1)
    slopes(1)
    project(1, 1, flipped)
    go_home(1, 0)
    pair_up(1, 1, (1, 2), (0, 3), (1, 3), (0, 4), (1, 4))
    go_home(1, 1)
    add_core(1, 1, 1)
    for piece in (2, 3, 4):
        go_home(0, piece)
        go_home(1, piece)

    def wait_home(t):
        wait_for(home.at[t, pl.ds(0, 63)], hgot_sem.at[t])
        pltpu.make_async_copy(frompair.at[t, 16, 1], home.at[t, e], hself_sem.at[t]).wait()

    wait_home(0)
    slot_out = (home[0].reshape(128, width).astype(F32) + bout[...]).astype(BF)
    comb = own_comb[...]
    disp = own_disp[...]
    comb_grad = nt(own_grad[...], slot_out)
    comb_term = comb * (comb_grad - jnp.sum(comb * comb_grad, axis=1, keepdims=True))
    wait_home(1)
    slot_in_grad = home[1].reshape(128, width)
    disp_grad = nt(own_tok[...], slot_in_grad)
    logit_grad = comb_term + disp * (disp_grad - jnp.sum(disp * disp_grad, axis=0, keepdims=True))
    result = mm(disp.astype(BF), slot_in_grad) + nt(logit_grad.astype(BF), keys[...])
    out_ref[...] = result.astype(BF)

    for t in range(2):
        wait_for(send.at[t, pl.ds(0, 39)], put_sem.at[t])
        wait_for(rows[t].at[0, pl.ds(0, 24)], fwd_sem.at[t])
        wait_for(rows[t].at[0], cput_sem.at[t])
        wait_for(fromcore.at[t], rput_sem.at[t])
        wait_for(frompair.at[t], zput_sem.at[t])
        wait_for(home.at[t, pl.ds(0, 63)], hput_sem.at[t])


def local(tokens, slot_keys, w_in, b_in, w_out, b_out, out_grad):
    images, positions, width = tokens.shape
    units = w_in.shape[2]
    slots = slot_keys.shape[1]
    anyspec = pl.BlockSpec(memory_space=pl.ANY)
    dma = pltpu.SemaphoreType.DMA
    out = pl.pallas_call(
        kernel,
        out_shape=pltpu.VMEM((positions, width), BF),
        in_specs=[anyspec] * 7,
        out_specs=pl.BlockSpec(memory_space=pltpu.VMEM),
        scratch_shapes=[
            pltpu.VMEM((positions, images, width), BF),
            pltpu.VMEM((positions, images, width), BF),
            pltpu.VMEM((positions * images, width), BF),
            pltpu.VMEM((positions * images, width), BF),
            pltpu.VMEM((width, slots), BF),
            pltpu.VMEM((2, width, units), BF),
            pltpu.VMEM((2, units, width), BF),
            pltpu.VMEM((2, units), F32),
            pltpu.VMEM((slots, width), F32),
            pltpu.VMEM((2, 64, 2, 2, width), BF),
            pltpu.VMEM((2, 64, 2, 2, width), BF),
            pltpu.VMEM((2, 64, 2, 2, width), BF),
            pltpu.VMEM((2, 128, units), F32),
            pltpu.VMEM((2, 128, units), BF),
            pltpu.VMEM((width // 128, 256, 128), F32),
            pltpu.VMEM((2, 2, 64, 2, 2, width), BF),
            pltpu.VMEM((2, 64, 2, 2, width), BF),
            pltpu.VMEM((2, 32, 2, 2, width), BF),
            pltpu.VMEM((2, 64, 2, width), BF),
            pltpu.VMEM((positions, width), BF),
            pltpu.VMEM((positions, width), BF),
            pltpu.VMEM((positions, slots), F32),
            pltpu.VMEM((positions, slots), F32),
            pltpu.VMEM((positions * images, slots), BF),
            pltpu.VMEM((positions * images, slots), BF),
            pltpu.VMEM((positions * images, slots), F32),
            pltpu.VMEM((2, units, width), BF),
            pltpu.VMEM((2, width, units), BF),
            dma((7,)), dma((2,)), dma((2, 4)), dma((2,)), dma((2,)), dma((2, 3)), dma((2,)), dma((2, 2)),
            dma((2,)), dma((2, 4)), dma((2,)), dma((2, 5)), dma((2,)), dma((2,)), dma((2,)),
        ],
        compiler_params=pltpu.CompilerParams(
            collective_id=0, has_side_effects=True, vmem_limit_bytes=58 * 1024 * 1024
        ),
        name="moe_input_grad",
    )(
        jnp.transpose(tokens, (1, 0, 2)), jnp.transpose(out_grad, (1, 0, 2)), slot_keys, w_in, b_in, w_out, b_out
    )
    return out[None]


def solution(mesh):
    return jax.shard_map(
        local,
        mesh=mesh,
        in_specs=(
            P("expert", None, None),
            P(),
            P("expert", None, "hidden"),
            P("expert", "hidden"),
            P("expert", "hidden", None),
            P(),
            P("expert", None, None),
        ),
        out_specs=P(("expert", "hidden"), None, None),
        check_vma=False,
    )
```
